256 devices in a mesh: dp: 16 (over x, y_hi, core), space: 16 (over y_lo, z).
Axes of the slice: x: 4, y: 4 (y_hi: 2, y_lo: 2; y = y_hi * 2 + y_lo), z: 8, core: 2. Of those that a mesh axis runs over, the one named last changes fastest.
Arguments:
- state_field: bfloat16 [16, 160, 320, 128], P('dp', 'space'), may hold values from -6 to 6
- cotangent: bfloat16 [16, 160, 320, 128], P('dp', 'space'), may hold values from -6 to 6
- fire_cells: int32 [16, 256], P('dp'), may hold values from 0 to 51199
- fire_kinds: int32 [16, 256], P('dp'), may hold values from 0 to 7
- fire_heat: float32 [16, 256], P('dp'), may hold values from 0.1 to 2
- forcing_table: bfloat16 [8, 128], replicated, may hold values from -6 to 6
- spectral_weight: bfloat16 [2, 80, 2, 128, 128], P(None, 'space'), may hold values from -0.375 to 0.375
- skip_weight: bfloat16 [128, 128], replicated, may hold values from -0.5 to 0.5
- up_weight: bfloat16 [128, 256], replicated, may hold values from -0.5 to 0.5
- down_weight: bfloat16 [256, 128], replicated, may hold values from -0.375 to 0.375
Outputs:
- grad_field: bfloat16 [16, 160, 320, 128], P('dp', 'space')
- grad_spectral: float32 [2, 80, 2, 128, 128], P(None, 'space')
- grad_skip: float32 [128, 128], replicated
- grad_up: float32 [128, 256], replicated
- grad_down: float32 [256, 128], replicated
- grad_table: float32 [8, 128], replicated
The draws below stay inside these ranges and needn't reach their ends.
All inputs are finite; a program needn't handle non-finite values.
Results may differ from the reference program's by a relative error of at most 0.03.
Values may be sent and summed in bfloat16 or wider, within the bound.
A program may use at most 128 MiB of HBM per device.

```python
import math
import jax
import jax.numpy as jnp
from jax import lax

LATITUDE_ROWS = 160
NLON = 320
LMAX = 160
ZONAL_MODES_KEPT = 160
CHAN = 128
HIDDEN_SIZE = 256
FORCE = 8
FIRES = 256
BATCH = 16


def set_ends(array, key, smallest, top_value):
    longest = array.shape.index(max(array.shape))
    spots = []
    for shift in (0, 1):
        where = [jax.random.randint(jax.random.fold_in(key, axis), (), 0, length) for axis, length in enumerate(array.shape)]
        where[longest] = (where[longest] + shift) % array.shape[longest]
        spots.append(tuple(where))
    return array.at[spots[0]].set(smallest).at[spots[1]].set(top_value)


def levels(stream_key, dims, pieces, low, top_value):
    def one(dim, parts):
        heights = jax.random.uniform(jax.random.fold_in(jax.random.fold_in(stream_key, 6), dim), (parts,), jnp.float32, low / len(pieces), top_value / len(pieces))
        return jnp.repeat(jnp.exp(heights), dims[dim] // parts).reshape((-1,) + (1,) * (len(dims) - dim - 1))

    gain = one(*pieces[0])
    for cut in pieces[1:]:
        gain = gain * one(*cut)
    return gain


def bell_draw(stream_key, extent, spread, limit, pieces=(), kind=jnp.bfloat16):
    entries = spread * jax.random.normal(stream_key, extent, jnp.float32)
    if pieces:
        entries = entries * levels(stream_key, extent, pieces, -0.22, 0.18)
    return jnp.clip(entries, -limit, limit).astype(kind)


def setup_inputs(seed: int = 0) -> dict:
    key_list = jax.random.split(jax.random.key(seed), 11)
    state_field = bell_draw(key_list[0], (BATCH, LATITUDE_ROWS, NLON, CHAN), 1.0, 6.0, ((0, 16), (1, 16)))
    cotangent = bell_draw(key_list[1], (BATCH, LATITUDE_ROWS, NLON, CHAN), 1.0, 6.0, ((0, 16), (1, 16)))
    fire_cells = set_ends(jax.random.randint(key_list[2], (BATCH, FIRES), 0, LATITUDE_ROWS * NLON), jax.random.fold_in(key_list[2], 1), 0, (LATITUDE_ROWS * NLON) - 1).astype(jnp.int32)
    fire_kinds = set_ends(jax.random.randint(key_list[3], (BATCH, FIRES), 0, FORCE), jax.random.fold_in(key_list[3], 1), 0, FORCE - 1).astype(jnp.int32)
    fire_heat = jnp.clip(jnp.exp(math.log(2.0) - 2.9957323 * jax.random.uniform(key_list[4], (BATCH, FIRES), jnp.float32) ** levels(key_list[4], (BATCH, FIRES), ((0, 16),), -0.2, 0.2)), 0.1, 2.0)
    forcing_table = bell_draw(key_list[5], (FORCE, CHAN), 1.0, 6.0)
    spectral_weight = bell_draw(key_list[6], (2, LMAX // 2, 2, CHAN, CHAN), (2 * CHAN) ** -0.5, 0.375, ((1, 16),))
    skip_weight = bell_draw(key_list[7], (CHAN, CHAN), CHAN ** -0.5, 0.5)
    up_weight = bell_draw(key_list[8], (CHAN, HIDDEN_SIZE), CHAN ** -0.5, 0.5)
    down_weight = bell_draw(key_list[9], (HIDDEN_SIZE, CHAN), HIDDEN_SIZE ** -0.5, 0.375)
    return dict(state_field=state_field, cotangent=cotangent, fire_cells=fire_cells, fire_kinds=fire_kinds, fire_heat=fire_heat, forcing_table=forcing_table, spectral_weight=spectral_weight, skip_weight=skip_weight, up_weight=up_weight, down_weight=down_weight)


EPSILON = 1e-06

def normalize(values):
    centre = values - lax.optimization_barrier(jnp.mean(values, axis=-1, keepdims=True))
    variance = lax.optimization_barrier(jnp.mean(centre * centre, axis=-1, keepdims=True))
    return centre * lax.rsqrt(variance + EPSILON)

def smooth(values):
    return jax.nn.gelu(values, approximate=True)

def fourier_tables(mode_ids, point_total):
    wavenumber = mode_ids.astype(jnp.int32)[:, None]
    position = jnp.arange(point_total, dtype=jnp.int32)[None, :]
    angles = 2.0 * jnp.pi / point_total * (wavenumber * position % point_total).astype(jnp.float32)
    cosine = jnp.cos(angles)
    sine_wave = jnp.sin(angles)
    factor = jnp.where(wavenumber == 0, 1.0, 2.0).astype(jnp.float32)
    analysis = jnp.stack([cosine / point_total, -sine_wave / point_total], axis=1).astype(jnp.bfloat16)
    synthesis = jnp.stack([factor * cosine, -factor * sine_wave], axis=1).astype(jnp.bfloat16)
    return (analysis, synthesis)

def legendre_tables(order_ids):
    mode_total = order_ids.shape[0]
    orders = order_ids.astype(jnp.float32)[:, None]
    colatitude = jnp.pi * (jnp.arange(LATITUDE_ROWS, dtype=jnp.int32).astype(jnp.float32) + 0.5) / LATITUDE_ROWS
    cos_lat = jnp.cos(colatitude)[None, :]
    sin_lat = jnp.sin(colatitude)[None, :]
    quadrature = 2.0 * jnp.pi * jnp.pi / LATITUDE_ROWS * sin_lat
    log_start = 0.5 * jnp.log((2.0 * orders + 1.0) / (4.0 * jnp.pi)) + 0.5 * (lax.lgamma(orders + 0.5) - lax.lgamma(orders + 1.0)) - 0.25 * jnp.log(jnp.pi)
    diagonal = jnp.exp(log_start + orders * jnp.log(sin_lat))

    def advance(state_pair, degree):
        previous, before = state_pair
        as_float = degree.astype(jnp.float32)
        upward = jnp.sqrt(jnp.maximum(4.0 * as_float * as_float - 1.0, 1.0) / jnp.maximum(as_float * as_float - orders * orders, 1.0))
        lower = as_float - 1.0
        downward = jnp.sqrt(jnp.maximum(lower * lower - orders * orders, 0.0) / jnp.maximum(4.0 * lower * lower - 1.0, 1.0))
        recurred = upward * (cos_lat * previous - downward * before)
        current = jnp.where(as_float == orders, diagonal, jnp.where(as_float > orders, recurred, 0.0))
        return ((current, previous), (current.astype(jnp.bfloat16), (current * quadrature).astype(jnp.bfloat16)))
    zeros_start = jnp.zeros((mode_total, LATITUDE_ROWS), jnp.float32)
    final_pair, tables = lax.scan(advance, (zeros_start, zeros_start), jnp.arange(LMAX, dtype=jnp.int32), unroll=16)
    return tables

def mix_matrix(weights):
    real_part = weights[:, 0]
    imag_part = weights[:, 1]
    top_rows = jnp.concatenate([real_part, imag_part], axis=-1)
    bottom = jnp.concatenate([-imag_part, real_part], axis=-1)
    return jnp.concatenate([top_rows, bottom], axis=1)

def mix_gradient(harmonic_coefficients, mixed_gradient):
    degree_count, mode_count, part_count, chan_count = harmonic_coefficients.shape
    flattened = harmonic_coefficients.reshape(degree_count, mode_count * part_count, chan_count)
    turned = jnp.stack([mixed_gradient[:, :, 1], -mixed_gradient[:, :, 0]], axis=2)
    paired = jnp.concatenate([mixed_gradient.reshape(flattened.shape), turned.reshape(flattened.shape)], axis=-1)
    outer_prod = jnp.einsum('lpr,lps->lrs', flattened.astype(jnp.float32), paired.astype(jnp.float32))
    return jnp.transpose(outer_prod.reshape(degree_count, chan_count, 2, chan_count), (0, 2, 1, 3))

def reference(state_field, cotangent, fire_cells, fire_kinds, fire_heat, forcing_table, spectral_weight, skip_weight, up_weight, down_weight):
    analysis, synthesis = fourier_tables(jnp.arange(ZONAL_MODES_KEPT, dtype=jnp.int32), NLON)
    plain_table, weighted = legendre_tables(jnp.arange(ZONAL_MODES_KEPT, dtype=jnp.int32))
    degree_weight = jnp.concatenate([spectral_weight[0], spectral_weight[1][::-1]], axis=0)
    mixing = mix_matrix(degree_weight)
    doubled_channels = 2 * CHAN
    analysis_wide = analysis.astype(jnp.float32)
    synthesis_wide = synthesis.astype(jnp.float32)
    plain_broad_table = plain_table.astype(jnp.float32)
    weighted_broad_table = weighted.astype(jnp.float32)
    mixing_broad_table = mixing.astype(jnp.float32)
    kind_range = jnp.arange(FORCE, dtype=jnp.int32)

    def one_sample(totals, inputs):
        field_in, incoming_grid, locations, kind_ids, heat_values = inputs
        flat_in = field_in.astype(jnp.float32).reshape(LATITUDE_ROWS * NLON, CHAN)
        selector = (kind_ids[:, None] == kind_range[None, :]).astype(jnp.float32)
        rows_added = heat_values[:, None] * jnp.dot(selector, forcing_table.astype(jnp.float32), precision=lax.Precision.HIGHEST)
        forced = flat_in.at[locations].add(rows_added)
        normed = normalize(forced).astype(jnp.bfloat16)
        spectrum_values = jnp.einsum('mpk,jkc->mjpc', analysis_wide, normed.reshape(LATITUDE_ROWS, NLON, CHAN).astype(jnp.float32)).astype(jnp.bfloat16)
        harmonic_coefficients = jnp.einsum('vbz,bzq->vbq', weighted_broad_table, spectrum_values.reshape(ZONAL_MODES_KEPT, LATITUDE_ROWS, doubled_channels).astype(jnp.float32)).astype(jnp.bfloat16)
        mixed_coefficients = jnp.einsum('acw,awf->acf', harmonic_coefficients.astype(jnp.float32), mixing_broad_table).astype(jnp.bfloat16)
        returned_rows = jnp.einsum('cfg,cft->fgt', plain_broad_table, mixed_coefficients.astype(jnp.float32)).astype(jnp.bfloat16)
        filtered = jnp.einsum('mpk,mjpc->jkc', synthesis_wide, returned_rows.reshape(ZONAL_MODES_KEPT, LATITUDE_ROWS, 2, CHAN).astype(jnp.float32)).reshape(LATITUDE_ROWS * NLON, CHAN)
        inner_sum = filtered + jnp.dot(normed, skip_weight, preferred_element_type=jnp.float32)
        activated = smooth(inner_sum)
        second = normalize(activated).astype(jnp.bfloat16)
        upper = jnp.dot(second, up_weight, preferred_element_type=jnp.float32)
        hidden = smooth(upper).astype(jnp.bfloat16)
        incoming = incoming_grid.reshape(LATITUDE_ROWS * NLON, CHAN)
        grad_hidden = jnp.dot(incoming, down_weight.T, preferred_element_type=jnp.float32)
        grad_down = jnp.dot(hidden.T, incoming, preferred_element_type=jnp.float32)
        grad_upper = jax.vjp(smooth, upper)[1](grad_hidden)[0].astype(jnp.bfloat16)
        grad_second = jnp.dot(grad_upper, up_weight.T, preferred_element_type=jnp.float32)
        grad_up = jnp.dot(second.T, grad_upper, preferred_element_type=jnp.float32)
        grad_activated = jax.vjp(normalize, activated)[1](grad_second)[0]
        grad_inner = jax.vjp(smooth, inner_sum)[1](grad_activated)[0].astype(jnp.bfloat16)
        grad_skip = jnp.dot(normed.T, grad_inner, preferred_element_type=jnp.float32)
        grad_normed = jnp.dot(grad_inner, skip_weight.T, preferred_element_type=jnp.float32)
        spectrum_gradient = jnp.einsum('mpk,jkc->mjpc', synthesis_wide, grad_inner.reshape(LATITUDE_ROWS, NLON, CHAN).astype(jnp.float32)).astype(jnp.bfloat16)
        mixed_gradient = jnp.einsum('vbz,bzq->vbq', plain_broad_table, spectrum_gradient.reshape(ZONAL_MODES_KEPT, LATITUDE_ROWS, doubled_channels).astype(jnp.float32)).astype(jnp.bfloat16)
        coefficient_gradient = jnp.einsum('dfb,dub->dfu', mixed_gradient.astype(jnp.float32), mixing_broad_table).astype(jnp.bfloat16)
        grad_degree = mix_gradient(harmonic_coefficients.reshape(LMAX, ZONAL_MODES_KEPT, 2, CHAN), mixed_gradient.reshape(LMAX, ZONAL_MODES_KEPT, 2, CHAN))
        gradient_returned = jnp.einsum('cfg,cft->fgt', weighted_broad_table, coefficient_gradient.astype(jnp.float32)).astype(jnp.bfloat16)
        grad_normed = grad_normed + jnp.einsum('mpk,mjpc->jkc', analysis_wide, gradient_returned.reshape(ZONAL_MODES_KEPT, LATITUDE_ROWS, 2, CHAN).astype(jnp.float32)).reshape(LATITUDE_ROWS * NLON, CHAN)
        grad_forced = incoming.astype(jnp.float32) + jax.vjp(normalize, forced)[1](grad_normed)[0]
        picked = grad_forced[locations]
        grad_table = jnp.dot(selector.T, heat_values[:, None] * picked, precision=lax.Precision.HIGHEST)
        grads = (grad_degree, grad_skip, grad_up, grad_down, grad_table)
        totals = jax.tree.map(jnp.add, totals, grads)
        return (totals, grad_forced.astype(jnp.bfloat16).reshape(LATITUDE_ROWS, NLON, CHAN))
    start_totals = (jnp.zeros((LMAX, 2, CHAN, CHAN), jnp.float32), jnp.zeros((CHAN, CHAN), jnp.float32), jnp.zeros((CHAN, HIDDEN_SIZE), jnp.float32), jnp.zeros((HIDDEN_SIZE, CHAN), jnp.float32), jnp.zeros((FORCE, CHAN), jnp.float32))
    totals, grad_field = lax.scan(one_sample, start_totals, (state_field, cotangent, fire_cells, fire_kinds, fire_heat))
    half_count = LMAX // 2
    grad_spectral = jnp.stack([totals[0][:half_count], totals[0][half_count:][::-1]], axis=0)
    return (grad_field, grad_spectral, totals[1], totals[2], totals[3], totals[4])
```

```python
import functools
import math

import jax
import jax.numpy as jnp
import ml_dtypes
import numpy as np
from jax import lax
from jax.experimental import pallas as pl
from jax.experimental.pallas import tpu as pltpu
from jax.sharding import PartitionSpec as P

ROWS = 160
NLON = 320
CHAN = 128
HIDDEN = 256
FORCE = 8
FIRES = 256
NS = 16
JL = 10
HB = 5
MM = 10
FULL = 200
HALF = 104
EPSILON = 1e-06
MESH = pl.DeviceIdType.MESH
F32 = jnp.float32
BF16 = jnp.bfloat16
ROOT = math.sqrt(2.0 / math.pi)
CUBIC = 0.044715


def constant_tables():
    device = np.arange(NS)
    low = 5 * device[None, :] + np.arange(HB)[:, None]
    orders = np.stack([low, ROWS - 1 - low])
    flat = orders.reshape(-1)
    angle = 2.0 * np.pi * ((flat[:, None] * np.arange(NLON)[None, :]) % NLON) / NLON
    cosine, sine = np.cos(angle), np.sin(angle)
    factor = np.where(flat == 0, 1.0, 2.0)[:, None]
    analysis = np.concatenate([cosine, -sine], axis=0) / NLON
    synthesis = np.concatenate([factor * cosine, -factor * sine], axis=0)
    theta = np.pi * (np.arange(ROWS) + 0.5) / ROWS
    start = np.zeros((NS, 16, 256))
    for d in range(NS):
        for r in range(MM):
            m = float(orders[r // HB, r % HB, d])
            log_start = (
                0.5 * math.log((2.0 * m + 1.0) / (4.0 * math.pi))
                + 0.5 * (math.lgamma(m + 0.5) - math.lgamma(m + 1.0))
                - 0.25 * math.log(math.pi)
            )
            start[d, r, :ROWS] = np.exp(log_start + m * np.log(np.sin(theta)))
    waves = np.zeros((8, 256))
    waves[0, :ROWS] = np.cos(theta)
    waves[1, :ROWS] = 2.0 * np.pi * np.pi / ROWS * np.sin(theta)
    narrow = lambda t: np.ascontiguousarray(t).astype(np.float32).astype(ml_dtypes.bfloat16)
    return (
        narrow(analysis),
        narrow(analysis.T),
        narrow(synthesis),
        narrow(synthesis.T),
        start.astype(np.float32),
        waves.astype(np.float32),
    )


def mm_nn(a, b):
    return lax.dot_general(a, b, (((1,), (0,)), ((), ())), preferred_element_type=F32)


def mm_nt(a, b):
    return lax.dot_general(a, b, (((1,), (1,)), ((), ())), preferred_element_type=F32)


def mm_tn(a, b):
    return lax.dot_general(a, b, (((0,), (0,)), ((), ())), preferred_element_type=F32)


def mm_exact(a, b):
    return lax.dot_general(
        a, b, (((1,), (0,)), ((), ())), preferred_element_type=F32, precision=lax.Precision.HIGHEST
    )


def mean(values):
    return jnp.sum(values, axis=-1, keepdims=True) * (1.0 / CHAN)


def normalize(values):
    centre = values - mean(values)
    scale = lax.rsqrt(mean(centre * centre) + EPSILON)
    return centre * scale, scale


def normalize_grad(unit, scale, grad):
    return scale * (grad - mean(grad) - unit * mean(grad * unit))


def gelu_parts(v):
    square = v * v
    t = jnp.tanh(ROOT * v * (1.0 + CUBIC * square))
    half = 0.5 * (1.0 + t)
    slope = half + 0.5 * v * (1.0 - t * t) * (ROOT * (1.0 + 3.0 * CUBIC * square))
    return v * half, slope


def wide(a, b):
    return jnp.concatenate([a, b], axis=-1)


def loop(count, body, start=0):
    def step(index, carry):
        body(index)
        return carry

    lax.fori_loop(start, count, step, 0)


def rounded(v):
    return v.astype(BF16).astype(F32)


def step_kernel(
    nd,
    x_ref,
    cot_ref,
    cells_row,
    cells_col,
    kinds_row,
    kinds_col,
    heat_row,
    heat_col,
    table_ref,
    weight_ref,
    skip_ref,
    up_ref,
    down_ref,
    ana_ref,
    anat_ref,
    syn_ref,
    synt_ref,
    start_ref,
    waves_ref,
    field_out,
    spectral_out,
    skip_out,
    up_out,
    down_out,
    table_out,
    unit,
    scale,
    normed,
    inner_grad,
    fire_t,
    taken,
    made,
    fsend,
    frecv,
    hsend,
    hrecv,
    extra,
    extra_back,
    t0,
    t1,
    plain,
    weighted,
    mix,
    coef,
    small,
    small_in,
    piece1,
    space_in,
    piece2,
    small_all,
    spec,
    spec_send,
    spec_in,
    spec_piece,
    spec_all,
    tab_mine,
    tab_space,
    tab_sum,
    tab_dp,
    ssem,
    rsem,
    dsend,
    drecv,
):
    me = lax.axis_index("space")
    dp = lax.axis_index("dp")
    pr = 640 // nd
    sr = 2560 // nd

    barrier = pltpu.get_barrier_semaphore()

    def greet_space(o):
        pl.semaphore_signal(barrier, 1, device_id={"space": lax.rem(me + o, NS)}, device_id_type=MESH)

    def greet_dp(o):
        pl.semaphore_signal(barrier, 1, device_id={"dp": lax.rem(dp + o, nd)}, device_id_type=MESH)

    loop(NS, greet_space, 1)
    if nd > 1:
        loop(nd, greet_dp, 1)

    def exchange_copy(send, recv, k, target, slot):
        return pltpu.make_async_remote_copy(
            src_ref=send.at[target],
            dst_ref=recv.at[slot],
            send_sem=ssem.at[k, target],
            recv_sem=rsem.at[k, slot],
            device_id={"space": target},
            device_id_type=MESH,
        )

    def send_blocks(send, recv, k, rows):
        def one(o):
            e = lax.rem(me + o, NS)
            send[e] = made[pl.ds(pl.multiple_of(e * rows, 8), rows), :].astype(BF16)
            exchange_copy(send, recv, k, e, me).start()

        loop(NS, one, 1)
        send[me] = made[pl.ds(pl.multiple_of(me * rows, 8), rows), :].astype(BF16)

    def take_blocks(send, recv, k, rows):
        taken[pl.ds(pl.multiple_of(me * rows, 8), rows), :] = send[me].astype(F32)

        def one(o):
            s = lax.rem(me + NS - o, NS)
            exchange_copy(send, recv, k, s, s).wait_recv()
            taken[pl.ds(pl.multiple_of(s * rows, 8), rows), :] = recv[s].astype(F32)

        def sent(o):
            s = lax.rem(me + o, NS)
            exchange_copy(send, recv, k, s, s).wait_send()

        loop(NS, one, 1)
        loop(NS, sent, 1)

    def spread(axis, count, mine, k, source_of, recv, start):
        def one(o):
            t = lax.rem(mine + o, count)
            slot = mine if start else t
            copy = pltpu.make_async_remote_copy(
                src_ref=source_of(t),
                dst_ref=recv.at[slot],
                send_sem=dsend.at[k, t],
                recv_sem=drecv.at[k, slot],
                device_id={axis: t},
                device_id_type=MESH,
            )
            if start:
                copy.start()
            else:
                copy.wait_recv()
                copy.wait_send()

        if count > 1:
            loop(count, one, 1)

    def total(recv, count):
        value = recv[0].astype(F32)
        for t in range(1, count):
            value = value + recv[t].astype(F32)
        return value

    lanes = lax.broadcasted_iota(jnp.int32, (FIRES, 128), 1)
    heat = jnp.broadcast_to(heat_col[...], (FIRES, 128))
    heat0 = rounded(heat)
    heat1 = rounded(heat - heat0)
    heat2 = heat - heat0 - heat1
    parts = jnp.where(lanes < 8, heat0, jnp.where(lanes < 16, heat1, heat2))
    chosen = (jnp.broadcast_to(kinds_col[...], (FIRES, 128)) == (lanes & 7)) & (lanes < 24)
    heats = jnp.where(chosen, parts, 0.0).astype(BF16)
    table_wide = table_ref[...].astype(F32)
    table3 = jnp.concatenate(
        [table_wide, table_wide, table_wide, jnp.zeros((104, CHAN), F32)], axis=0
    )

    def to_orders(j, table, row):
        spectrum = mm_nn(table[...], row)
        for r in range(2 * MM):
            made[pl.ds(j * (2 * MM) + r, NS, stride=FULL), :] = spectrum[r * NS : (r + 1) * NS]

    def from_orders(j, table):
        pieces = [taken[pl.ds(j * (2 * MM) + r, NS, stride=FULL), :] for r in range(2 * MM)]
        return mm_nn(table[...], jnp.concatenate(pieces, axis=0).astype(BF16))

    def field_row(j):
        base = (me * JL + j) * NLON
        cells = lax.broadcasted_iota(jnp.int32, (NLON, FIRES), 0) + base
        hot = jnp.where(cells == cells_row[...], 1.0, 0.0).astype(BF16)
        added = mm_exact(mm_nn(hot, heats), table3)
        value, factor = normalize(x_ref[j].astype(F32) + added)
        unit[j] = value
        scale[j] = jnp.broadcast_to(factor, (NLON, CHAN))
        narrow = value.astype(BF16)
        normed[j] = narrow
        to_orders(j, ana_ref, narrow)

    loop(JL, field_row)
    pl.semaphore_wait(barrier, (NS - 1) + (nd - 1))
    send_blocks(fsend.at[0], frecv.at[0], 0, FULL)

    row16 = lax.broadcasted_iota(jnp.int32, (16, 128), 0)
    order = jnp.where(row16 >= HB, ROWS - 1 - 5 * me - (row16 - HB), 5 * me + row16).astype(F32)
    order2 = order * order
    cos0 = jnp.broadcast_to(waves_ref[0:1, 0:128], (16, 128))
    cos1 = jnp.broadcast_to(waves_ref[0:1, 128:256], (16, 128))

    def advance(l, carry):
        p0, p1, b0, b1 = carry
        lf = jnp.full((16, 128), l, jnp.int32).astype(F32)
        lower = lf - 1.0
        upward = jnp.sqrt(
            jnp.maximum(4.0 * lf * lf - 1.0, 1.0) / jnp.maximum(lf * lf - order2, 1.0)
        )
        downward = jnp.sqrt(
            jnp.maximum(lower * lower - order2, 0.0) / jnp.maximum(4.0 * lower * lower - 1.0, 1.0)
        )
        first = start_ref[me]
        at_start = lf == order
        above = lf > order
        c0 = jnp.where(
            at_start, first[:, 0:128], jnp.where(above, upward * (cos0 * p0 - downward * b0), 0.0)
        )
        c1 = jnp.where(
            at_start, first[:, 128:256], jnp.where(above, upward * (cos1 * p1 - downward * b1), 0.0)
        )
        upper_half = l // 80
        q = l + upper_half * (ROWS - 1 - 2 * l)
        place = (upper_half * HB + q % HB) * NS + q // HB
        t0[pl.ds(place, 16, stride=ROWS), :] = c0
        t1[pl.ds(place, 16, stride=ROWS), :] = c1
        return (c0, c1, p0, p1)

    blank = start_ref[me][:, 0:128] * 0.0
    lax.fori_loop(0, ROWS, advance, (blank, blank, blank, blank))

    def narrow_tables(r):
        at = pl.ds(pl.multiple_of(r * ROWS, 8), ROWS)
        values = wide(t0[at, :], t1[at, :])
        plain[r] = values.astype(BF16)
        weighted[r] = (values * waves_ref[1:2, :]).astype(BF16)

    loop(MM, narrow_tables)

    def build_mix(g):
        real = weight_ref[2 * g]
        imag = weight_ref[2 * g + 1]
        mix[g, 0:128, 0:128] = real
        mix[g, 0:128, 128:256] = imag
        mix[g, 128:256, 0:128] = -imag
        mix[g, 128:256, 128:256] = real

    loop(2 * HB, build_mix)

    rows32 = lax.broadcasted_iota(jnp.int32, (32, FIRES), 0)
    hr = jnp.broadcast_to(heat_row[...], (32, FIRES))
    hr0 = rounded(hr)
    hr1 = rounded(hr - hr0)
    hr2 = hr - hr0 - hr1
    part = jnp.where(rows32 < 8, hr0, jnp.where(rows32 < 16, hr1, hr2))
    pick = (jnp.broadcast_to(kinds_row[...], (32, FIRES)) == (rows32 & 7)) & (rows32 < 24)
    heats_t = jnp.where(pick, part, 0.0).astype(BF16)

    def fire_columns(j):
        base = (me * JL + j) * NLON
        cells = lax.broadcasted_iota(jnp.int32, (FIRES, NLON), 1) + base
        hot = jnp.where(cells == cells_col[...], 1.0, 0.0).astype(BF16)
        fire_t[j] = mm_nn(heats_t, hot)

    loop(JL, fire_columns)

    def analyse(fk, k_in, hk, k_out, table):
        take_blocks(fsend.at[fk], frecv.at[fk], k_in, FULL)

        def field_of(r):
            a = taken[pl.ds(r, ROWS, stride=2 * MM), :]
            b = taken[pl.ds(MM + r, ROWS, stride=2 * MM), :]
            return wide(a, b).astype(BF16)

        def one(i):
            low = mm_nn(table[i][:, 0:ROWS], field_of(i))
            high = mm_nn(table[HB + i][:, 0:ROWS], field_of(HB + i))
            for p in range(2):
                lane = slice(p * 128, (p + 1) * 128)
                for ii in range(HB):
                    ll = low[ii * NS : (ii + 1) * NS, lane]
                    lh = low[(HB + ii) * NS : (HB + ii + 1) * NS, lane]
                    hh = high[(HB + ii) * NS : (HB + ii + 1) * NS, lane]
                    at = p * 50 + i * HB + ii
                    made[pl.ds(at, NS, stride=HALF), :] = lh
                    made[pl.ds(at + 25, NS, stride=HALF), :] = jnp.where(row16 >= me, ll, hh)
                    extra[pl.ds(p * 32 + i * HB + ii, NS, stride=64), :] = rounded(hh)

        loop(HB, one)
        send_blocks(hsend.at[hk], hrecv.at[hk], k_out, HALF)

    row80 = lax.broadcasted_iota(jnp.int32, (80, 256), 0) & 15
    from_low = row80 <= me

    def mix_degrees(hk_in, k_in, hk_out, k_out, backward):
        take_blocks(hsend.at[hk_in], hrecv.at[hk_in], k_in, HALF)
        product = mm_nt if backward else mm_nn
        for ii in range(HB):

            def gather(slot):
                pieces = []
                for i in range(HB):
                    at = slot * 25 + i * HB + ii
                    pieces.append(
                        wide(
                            taken[pl.ds(at, NS, stride=HALF), :],
                            taken[pl.ds(50 + at, NS, stride=HALF), :],
                        )
                    )
                return jnp.concatenate(pieces, axis=0)

            own = wide(
                extra[pl.ds(me * 64 + ii, 8, stride=HB), :],
                extra[pl.ds(me * 64 + 32 + ii, 8, stride=HB), :],
            )
            own = jnp.where(lax.broadcasted_iota(jnp.int32, (8, 256), 0) < HB, own, 0.0)
            second = gather(1)
            rows = jnp.concatenate(
                [gather(0), second, own, jnp.zeros((8, 256), F32)], axis=0
            )
            narrow = rows.astype(BF16)
            second_narrow = second.astype(BF16)
            high = product(narrow, mix[HB + ii])
            low = product(second_narrow, mix[ii])
            mixed_second = jnp.where(from_low, low, high[80:160])
            for p in range(2):
                lane = slice(p * 128, (p + 1) * 128)
                for i in range(HB):
                    at = p * 50 + ii * HB + i
                    made[pl.ds(at, NS, stride=HALF), :] = high[i * NS : (i + 1) * NS, lane]
                    made[pl.ds(at + 25, NS, stride=HALF), :] = mixed_second[
                        i * NS : (i + 1) * NS, lane
                    ]
                extra_back[p * 32 + ii * HB : p * 32 + ii * HB + 8, :] = rounded(high[160:168, lane])
            if backward:
                kept = coef[ii].astype(F32)
                kept_second = kept[80:160]
                kept_high = jnp.concatenate(
                    [kept[0:80], jnp.where(from_low, 0.0, kept_second), kept[160:176]], axis=0
                )
                kept_low = jnp.where(from_low, kept_second, 0.0)
                grad_high = mm_tn(kept_high.astype(BF16), narrow)
                grad_low = mm_tn(kept_low.astype(BF16), second_narrow)
                for half, grad in ((0, grad_low), (1, grad_high)):
                    at = (half * HB + ii) * 256
                    spec[at : at + 128, :] = grad[0:128, 0:128] + grad[128:256, 128:256]
                    spec[at + 128 : at + 256, :] = grad[0:128, 128:256] - grad[128:256, 0:128]
            else:
                coef[ii] = narrow
        send_blocks(hsend.at[hk_out], hrecv.at[hk_out], k_out, HALF)

    def synthesise(hk, k_in, fk, k_out, table):
        take_blocks(hsend.at[hk], hrecv.at[hk], k_in, HALF)

        def one(i):
            def rows_of(slot, ii):
                at = slot * 25 + ii * HB + i
                return wide(
                    taken[pl.ds(at, NS, stride=HALF), :], taken[pl.ds(50 + at, NS, stride=HALF), :]
                )

            seconds = [rows_of(1, ii) for ii in range(HB)]
            firsts = [rows_of(0, ii) for ii in range(HB)]
            mine = lax.broadcasted_iota(jnp.int32, (NS, 256), 0) == me
            highs = []
            for ii in range(HB):
                own = wide(
                    extra_back[pl.ds(ii * HB + i, 1), :], extra_back[pl.ds(32 + ii * HB + i, 1), :]
                )
                highs.append(jnp.where(mine, jnp.broadcast_to(own, (NS, 256)), seconds[ii]))
            low = mm_tn(
                table[i][:, 0:ROWS], jnp.concatenate(seconds + firsts, axis=0).astype(BF16)
            )
            high = mm_tn(
                table[HB + i][:, 0:ROWS], jnp.concatenate(seconds + highs, axis=0).astype(BF16)
            )
            made[pl.ds(i, ROWS, stride=2 * MM), :] = low[:, 0:128]
            made[pl.ds(MM + i, ROWS, stride=2 * MM), :] = low[:, 128:256]
            made[pl.ds(HB + i, ROWS, stride=2 * MM), :] = high[:, 0:128]
            made[pl.ds(MM + HB + i, ROWS, stride=2 * MM), :] = high[:, 128:256]

        loop(HB, one)
        send_blocks(fsend.at[fk], frecv.at[fk], k_out, FULL)

    analyse(0, 0, 0, 1, weighted)
    mix_degrees(0, 1, 1, 2, False)
    synthesise(1, 2, 1, 3, plain)

    take_blocks(fsend.at[1], frecv.at[1], 3, FULL)
    small[...] = jnp.zeros((640, CHAN), F32)

    def middle_row(j):
        row = normed[j]
        inner = from_orders(j, synt_ref) + mm_nn(row, skip_ref[...])
        activated, inner_slope = gelu_parts(inner)
        second, factor = normalize(activated)
        narrow = second.astype(BF16)
        upper = mm_nn(narrow, up_ref[...])
        hidden, slope = gelu_parts(upper)
        incoming = cot_ref[j]
        grad_upper = (mm_nt(incoming, down_ref[...]) * slope).astype(BF16)
        grad_second = mm_nt(grad_upper, up_ref[...])
        small[384:640, :] += mm_tn(hidden.astype(BF16), incoming)
        grad_up = mm_tn(narrow, grad_upper)
        small[128:256, :] += grad_up[:, 0:128]
        small[256:384, :] += grad_up[:, 128:256]
        grad_inner = (normalize_grad(second, factor, grad_second) * inner_slope).astype(BF16)
        small[0:128, :] += mm_tn(row, grad_inner)
        inner_grad[j] = grad_inner
        to_orders(j, syn_ref, grad_inner)

    loop(JL, middle_row)
    send_blocks(fsend.at[2], frecv.at[2], 4, FULL)

    def small_source(t):
        return small.at[pl.ds(pl.multiple_of(t * pr, 8), pr), :]

    spread("dp", nd, dp, 0, small_source, small_in, True)
    small_in[dp] = small[pl.ds(pl.multiple_of(dp * pr, 8), pr), :]

    analyse(2, 4, 2, 5, plain)

    spread("dp", nd, dp, 0, small_source, small_in, False)
    piece1[...] = total(small_in, nd)
    spread("space", NS, me, 1, lambda t: piece1, space_in, True)
    space_in[me] = piece1[...]

    mix_degrees(2, 5, 3, 6, True)

    spread("space", NS, me, 1, lambda t: piece1, space_in, False)
    piece2[...] = total(space_in, NS)
    spread("dp", nd, dp, 2, lambda t: piece2, small_all, True)
    small_all[dp] = piece2[...]

    def narrow_spec(t):
        spec_send[t] = spec[pl.ds(pl.multiple_of(t * sr, 16), sr), :].astype(BF16)

    loop(nd, narrow_spec)
    spread("dp", nd, dp, 3, lambda t: spec_send.at[t], spec_in, True)
    spec_in[dp] = spec_send[dp]

    synthesise(3, 6, 3, 7, weighted)

    spread("dp", nd, dp, 3, lambda t: spec_send.at[t], spec_in, False)
    spec_piece[...] = total(spec_in, nd).astype(BF16)
    spread("dp", nd, dp, 4, lambda t: spec_piece, spec_all, True)
    spec_all[dp] = spec_piece[...]

    take_blocks(fsend.at[3], frecv.at[3], 7, FULL)
    tab_mine[...] = jnp.zeros((32, CHAN), F32)

    def last_row(j):
        grad_normed = from_orders(j, anat_ref) + mm_nt(inner_grad[j], skip_ref[...])
        grad = cot_ref[j].astype(F32) + normalize_grad(unit[j], scale[j], grad_normed)
        field_out[j] = grad.astype(BF16)
        tab_mine[...] += mm_exact(fire_t[j], grad)

    loop(JL, last_row)
    tab_mine[0:8, :] = tab_mine[0:8, :] + tab_mine[8:16, :] + tab_mine[16:24, :]
    spread("space", NS, me, 5, lambda t: tab_mine.at[0:8], tab_space, True)
    tab_space[me] = tab_mine[0:8, :]

    spread("dp", nd, dp, 2, lambda t: piece2, small_all, False)
    flat_small = [small_all[t] for t in range(nd)]
    flat_small = jnp.concatenate(flat_small, axis=0)
    skip_out[...] = flat_small[0:128]
    up_out[:, 0:128] = flat_small[128:256]
    up_out[:, 128:256] = flat_small[256:384]
    down_out[...] = flat_small[384:640]
    spread("dp", nd, dp, 4, lambda t: spec_piece, spec_all, False)

    def widen_spec(t):
        spectral_out[pl.ds(pl.multiple_of(t * sr, 16), sr), :] = spec_all[t].astype(F32)

    loop(nd, widen_spec)

    spread("space", NS, me, 5, lambda t: tab_mine.at[0:8], tab_space, False)
    tab_sum[...] = total(tab_space, NS)
    spread("dp", nd, dp, 6, lambda t: tab_sum, tab_dp, True)
    tab_dp[dp] = tab_sum[...]
    spread("dp", nd, dp, 6, lambda t: tab_sum, tab_dp, False)
    table_out[...] = total(tab_dp, nd)


def shards(
    nd,
    state_field,
    cotangent,
    fire_cells,
    fire_kinds,
    fire_heat,
    forcing_table,
    spectral_weight,
    skip_weight,
    up_weight,
    down_weight,
):
    ana, anat, syn, synt, start, waves = (jnp.asarray(t) for t in constant_tables())
    pr, sr = 640 // nd, 2560 // nd
    operands = (
        state_field[0],
        cotangent[0],
        fire_cells,
        fire_cells.reshape(FIRES, 1),
        fire_kinds,
        fire_kinds.reshape(FIRES, 1),
        fire_heat,
        fire_heat.reshape(FIRES, 1),
        forcing_table,
        spectral_weight.reshape(4 * HB, CHAN, CHAN),
        skip_weight,
        up_weight,
        down_weight,
        ana,
        anat,
        syn,
        synt,
        start,
        waves,
    )
    vmem = pl.BlockSpec(memory_space=pltpu.VMEM)
    out_shape = (
        jax.ShapeDtypeStruct((JL, NLON, CHAN), BF16),
        jax.ShapeDtypeStruct((2560, CHAN), F32),
        jax.ShapeDtypeStruct((CHAN, CHAN), F32),
        jax.ShapeDtypeStruct((CHAN, HIDDEN), F32),
        jax.ShapeDtypeStruct((HIDDEN, CHAN), F32),
        jax.ShapeDtypeStruct((FORCE, CHAN), F32),
    )
    scratch = [
        pltpu.VMEM((JL, NLON, CHAN), F32),
        pltpu.VMEM((JL, NLON, CHAN), F32),
        pltpu.VMEM((JL, NLON, CHAN), BF16),
        pltpu.VMEM((JL, NLON, CHAN), BF16),
        pltpu.VMEM((JL, 32, NLON), F32),
        pltpu.VMEM((NS * FULL, CHAN), F32),
        pltpu.VMEM((NS * FULL, CHAN), F32),
        pltpu.VMEM((4, NS, FULL, CHAN), BF16),
        pltpu.VMEM((4, NS, FULL, CHAN), BF16),
        pltpu.VMEM((4, NS, HALF, CHAN), BF16),
        pltpu.VMEM((4, NS, HALF, CHAN), BF16),
        pltpu.VMEM((NS * 64 + 16, CHAN), F32),
        pltpu.VMEM((72, CHAN), F32),
        pltpu.VMEM((16 * ROWS, 128), F32),
        pltpu.VMEM((16 * ROWS, 128), F32),
        pltpu.VMEM((MM, ROWS, 256), BF16),
        pltpu.VMEM((MM, ROWS, 256), BF16),
        pltpu.VMEM((2 * HB, 256, 256), BF16),
        pltpu.VMEM((HB, 176, 256), BF16),
        pltpu.VMEM((640, CHAN), F32),
        pltpu.VMEM((nd, pr, CHAN), F32),
        pltpu.VMEM((pr, CHAN), F32),
        pltpu.VMEM((NS, pr, CHAN), F32),
        pltpu.VMEM((pr, CHAN), F32),
        pltpu.VMEM((nd, pr, CHAN), F32),
        pltpu.VMEM((2560, CHAN), F32),
        pltpu.VMEM((nd, sr, CHAN), BF16),
        pltpu.VMEM((nd, sr, CHAN), BF16),
        pltpu.VMEM((sr, CHAN), BF16),
        pltpu.VMEM((nd, sr, CHAN), BF16),
        pltpu.VMEM((32, CHAN), F32),
        pltpu.VMEM((NS, FORCE, CHAN), F32),
        pltpu.VMEM((FORCE, CHAN), F32),
        pltpu.VMEM((nd, FORCE, CHAN), F32),
        pltpu.SemaphoreType.DMA((8, NS)),
        pltpu.SemaphoreType.DMA((8, NS)),
        pltpu.SemaphoreType.DMA((7, NS)),
        pltpu.SemaphoreType.DMA((7, NS)),
    ]
    field, spectral, skip, up, down, table = pl.pallas_call(
        functools.partial(step_kernel, nd),
        out_shape=out_shape,
        in_specs=[vmem] * len(operands),
        out_specs=(vmem,) * len(out_shape),
        scratch_shapes=scratch,
        compiler_params=pltpu.CompilerParams(
            collective_id=0, has_side_effects=True, vmem_limit_bytes=60 << 20
        ),
        name="step",
    )(*operands)
    return (field[None], spectral.reshape(spectral_weight.shape), skip, up, down, table)


def solution(mesh):
    return jax.shard_map(
        functools.partial(shards, mesh.shape["dp"]),
        mesh=mesh,
        in_specs=(
            P("dp", "space", None, None),
            P("dp", "space", None, None),
            P("dp", None),
            P("dp", None),
            P("dp", None),
            P(),
            P(None, "space", None, None, None),
            P(),
            P(),
            P(),
        ),
        out_specs=(
            P("dp", "space", None, None),
            P(None, "space", None, None, None),
            P(),
            P(),
            P(),
            P(),
        ),
        check_vma=False,
    )
```

```python
import functools
import math

import jax
import jax.numpy as jnp
import ml_dtypes
import numpy as np
from jax import lax
from jax.experimental import pallas as pl
from jax.experimental.pallas import tpu as pltpu
from jax.sharding import PartitionSpec as P

ROWS = 160
NLON = 320
CHAN = 128
HIDDEN = 256
FORCE = 8
FIRES = 256
NS = 16
JL = 10
HB = 5
MM = 10
FULL = 200
PAIR = 40
PARTS = ((0, 2, 40), (2, 3, 64))
OWNERS = 5
EPSILON = 1e-06
MESH = pl.DeviceIdType.MESH
F32 = jnp.float32
BF16 = jnp.bfloat16
ROOT = math.sqrt(2.0 / math.pi)
CUBIC = 0.044715


def constant_tables():
    device = np.arange(NS)
    low = 5 * device[None, :] + np.arange(HB)[:, None]
    orders = np.stack([low, ROWS - 1 - low])
    flat = orders.reshape(-1)
    angle = 2.0 * np.pi * ((flat[:, None] * np.arange(NLON)[None, :]) % NLON) / NLON
    cosine, sine = np.cos(angle), np.sin(angle)
    factor = np.where(flat == 0, 1.0, 2.0)[:, None]
    analysis = np.concatenate([cosine, -sine], axis=0) / NLON
    synthesis = np.concatenate([factor * cosine, -factor * sine], axis=0)
    theta = np.pi * (np.arange(ROWS) + 0.5) / ROWS
    start = np.zeros((NS, 16, 256))
    for d in range(NS):
        for r in range(MM):
            m = float(orders[r // HB, r % HB, d])
            log_start = (
                0.5 * math.log((2.0 * m + 1.0) / (4.0 * math.pi))
                + 0.5 * (math.lgamma(m + 0.5) - math.lgamma(m + 1.0))
                - 0.25 * math.log(math.pi)
            )
            start[d, r, :ROWS] = np.exp(log_start + m * np.log(np.sin(theta)))
    waves = np.zeros((8, 256))
    waves[0, :ROWS] = np.cos(theta)
    waves[1, :ROWS] = 2.0 * np.pi * np.pi / ROWS * np.sin(theta)
    narrow = lambda t: np.ascontiguousarray(t).astype(np.float32).astype(ml_dtypes.bfloat16)
    return (
        narrow(analysis),
        narrow(analysis.T),
        narrow(synthesis),
        narrow(synthesis.T),
        start.astype(np.float32),
        waves.astype(np.float32),
    )


def mm_nn(a, b):
    return lax.dot_general(a, b, (((1,), (0,)), ((), ())), preferred_element_type=F32)


def mm_nt(a, b):
    return lax.dot_general(a, b, (((1,), (1,)), ((), ())), preferred_element_type=F32)


def mm_tn(a, b):
    return lax.dot_general(a, b, (((0,), (0,)), ((), ())), preferred_element_type=F32)


def mm_exact(a, b):
    return lax.dot_general(
        a, b, (((1,), (0,)), ((), ())), preferred_element_type=F32, precision=lax.Precision.HIGHEST
    )


def mean(values):
    return jnp.sum(values, axis=-1, keepdims=True) * (1.0 / CHAN)


def normalize(values):
    centre = values - mean(values)
    scale = lax.rsqrt(mean(centre * centre) + EPSILON)
    return centre * scale, scale


def normalize_grad(unit, scale, grad):
    return scale * (grad - mean(grad) - unit * mean(grad * unit))


def gelu_parts(v):
    square = v * v
    t = jnp.tanh(ROOT * v * (1.0 + CUBIC * square))
    half = 0.5 * (1.0 + t)
    slope = half + 0.5 * v * (1.0 - t * t) * (ROOT * (1.0 + 3.0 * CUBIC * square))
    return v * half, slope


def wide(a, b):
    return jnp.concatenate([a, b], axis=-1)


def loop(count, body, start=0):
    def step(index, carry):
        body(index)
        return carry

    lax.fori_loop(start, count, step, 0)


def rounded(v):
    return v.astype(BF16).astype(F32)


def step_kernel(
    nd,
    x_ref,
    cot_ref,
    cells_row,
    kinds_row,
    heat_row,
    table_ref,
    weight_ref,
    skip_ref,
    up_ref,
    down_ref,
    ana_ref,
    anat_ref,
    syn_ref,
    synt_ref,
    start_ref,
    waves_ref,
    field_out,
    spectral_out,
    skip_out,
    up_out,
    down_out,
    table_out,
    unit,
    scale,
    normed,
    inner_grad,
    fire_g,
    fire_t,
    taken,
    made,
    fsend,
    frecv,
    hsend_a,
    hrecv_a,
    hsend_b,
    hrecv_b,
    extra,
    back_a,
    back_b,
    t0,
    t1,
    plain,
    weighted,
    mix,
    coef_a,
    coef_b,
    grad_a,
    grad_b,
    small,
    small_in,
    piece1,
    own_in,
    own_sum,
    piece2,
    small_all,
    spec,
    spec_send,
    spec_in,
    spec_piece,
    spec_all,
    tab_mine,
    tab_space,
    tab_sum,
    tab_dp,
    ssem,
    rsem,
    dsend,
    drecv,
):
    me = lax.axis_index("space")
    dp = lax.axis_index("dp")
    pr = 640 // nd
    sr = 2560 // nd
    og = pr // OWNERS
    hsend, hrecv = (hsend_a, hsend_b), (hrecv_a, hrecv_b)
    back, coef, grad_rows = (back_a, back_b), (coef_a, coef_b), (grad_a, grad_b)

    barrier = pltpu.get_barrier_semaphore()

    def greet_space(o):
        pl.semaphore_signal(barrier, 1, device_id={"space": lax.rem(me + o, NS)}, device_id_type=MESH)

    def greet_dp(o):
        pl.semaphore_signal(barrier, 1, device_id={"dp": lax.rem(dp + o, nd)}, device_id_type=MESH)

    loop(NS, greet_space, 1)
    if nd > 1:
        loop(nd, greet_dp, 1)

    def exchange(send, recv, at, k, source):
        count = at.size

        def one(o):
            e = lax.rem(me + o, NS)
            send[e, at, :] = made[pl.ds(pl.multiple_of(source(e), 8), count), :].astype(BF16)
            pltpu.make_async_remote_copy(
                src_ref=send.at[e, at],
                dst_ref=recv.at[me, at],
                send_sem=ssem.at[k],
                recv_sem=rsem.at[k],
                device_id={"space": e},
                device_id_type=MESH,
            ).start()

        loop(NS, one, 1)
        recv[me, at, :] = made[pl.ds(pl.multiple_of(source(me), 8), count), :].astype(BF16)

    def whole(send, recv, at, k):
        return pltpu.make_async_remote_copy(
            src_ref=send.at[pl.ds(0, NS - 1), at],
            dst_ref=recv.at[pl.ds(0, NS - 1), at],
            send_sem=ssem.at[k],
            recv_sem=rsem.at[k],
            device_id={"space": lax.rem(me + 1, NS)},
            device_id_type=MESH,
        )

    def arrived(send, recv, at, k, target):
        whole(send, recv, at, k).wait_recv()

        def one(s):
            taken[pl.ds(pl.multiple_of(target(s), 8), at.size), :] = recv[s, at, :].astype(F32)

        loop(NS, one)

    def spread(axis, count, mine, k, source_of, recv, start):
        if count == 1:
            return
        if not start:
            done = pltpu.make_async_remote_copy(
                src_ref=recv.at[pl.ds(0, count - 1)],
                dst_ref=recv.at[pl.ds(0, count - 1)],
                send_sem=dsend.at[k],
                recv_sem=drecv.at[k],
                device_id={axis: lax.rem(mine + 1, count)},
                device_id_type=MESH,
            )
            done.wait_recv()
            done.wait_send()
            return

        def one(o):
            t = lax.rem(mine + o, count)
            pltpu.make_async_remote_copy(
                src_ref=source_of(t),
                dst_ref=recv.at[mine],
                send_sem=dsend.at[k],
                recv_sem=drecv.at[k],
                device_id={axis: t},
                device_id_type=MESH,
            ).start()

        loop(count, one, 1)

    def total(recv, count):
        value = recv[0].astype(F32)
        for t in range(1, count):
            value = value + recv[t].astype(F32)
        return value

    def column(row):
        return jnp.broadcast_to(row.astype(F32), (128, FIRES)).T

    lanes = lax.broadcasted_iota(jnp.int32, (FIRES, 128), 1)
    heat = column(heat_row[...])
    heat0 = rounded(heat)
    heat1 = rounded(heat - heat0)
    heat2 = heat - heat0 - heat1
    parts = jnp.where(lanes < 8, heat0, jnp.where(lanes < 16, heat1, heat2))
    chosen = (column(kinds_row[...]) == (lanes & 7).astype(F32)) & (lanes < 24)
    heats = jnp.where(chosen, parts, 0.0).astype(BF16)
    table_wide = table_ref[...].astype(F32)
    table3 = jnp.concatenate(
        [table_wide, table_wide, table_wide, jnp.zeros((104, CHAN), F32)], axis=0
    )

    def field_row(j):
        base = (me * JL + j) * NLON
        cells = lax.broadcasted_iota(jnp.int32, (NLON, FIRES), 0) + base
        hot = jnp.where(cells == cells_row[...], 1.0, 0.0).astype(BF16)
        fires = mm_nn(hot, heats)
        fire_g[j] = fires
        value, factor = normalize(x_ref[j].astype(F32) + mm_exact(fires, table3))
        unit[j] = value
        scale[j] = jnp.broadcast_to(factor, (NLON, CHAN))
        narrow = value.astype(BF16)
        normed[j] = narrow
        spectrum = mm_nn(ana_ref[...], narrow)
        for p in range(2):
            for h in range(2):
                for i in range(HB):
                    r = (p * MM + h * HB + i) * NS
                    made[pl.ds(i * PAIR + j * 4 + p * 2 + h, NS, stride=FULL), :] = spectrum[r : r + NS]

    loop(JL, field_row)
    pl.semaphore_wait(barrier, (NS - 1) + (nd - 1))
    first_at = [pl.ds(first * PAIR, count * PAIR) for first, count, _ in PARTS]
    for c, at in enumerate(first_at):
        exchange(fsend.at[0], frecv.at[0], at, c, lambda e: e * FULL + at.start)

    row16 = lax.broadcasted_iota(jnp.int32, (16, 128), 0)
    order = jnp.where(row16 >= HB, ROWS - 1 - 5 * me - (row16 - HB), 5 * me + row16).astype(F32)
    order2 = order * order
    cos0 = jnp.broadcast_to(waves_ref[0:1, 0:128], (16, 128))
    cos1 = jnp.broadcast_to(waves_ref[0:1, 128:256], (16, 128))

    def advance(l, carry):
        p0, p1, b0, b1 = carry
        lf = jnp.full((16, 128), l, jnp.int32).astype(F32)
        lower = lf - 1.0
        upward = jnp.sqrt(
            jnp.maximum(4.0 * lf * lf - 1.0, 1.0) / jnp.maximum(lf * lf - order2, 1.0)
        )
        downward = jnp.sqrt(
            jnp.maximum(lower * lower - order2, 0.0) / jnp.maximum(4.0 * lower * lower - 1.0, 1.0)
        )
        first = start_ref[me]
        at_start = lf == order
        above = lf > order
        c0 = jnp.where(
            at_start, first[:, 0:128], jnp.where(above, upward * (cos0 * p0 - downward * b0), 0.0)
        )
        c1 = jnp.where(
            at_start, first[:, 128:256], jnp.where(above, upward * (cos1 * p1 - downward * b1), 0.0)
        )
        upper_half = l // 80
        q = l + upper_half * (ROWS - 1 - 2 * l)
        place = (upper_half * HB + q % HB) * NS + q // HB
        t0[pl.ds(place, 16, stride=ROWS), :] = c0
        t1[pl.ds(place, 16, stride=ROWS), :] = c1
        return (c0, c1, p0, p1)

    blank = start_ref[me][:, 0:128] * 0.0
    lax.fori_loop(0, ROWS, advance, (blank, blank, blank, blank))

    def narrow_tables(r):
        at = pl.ds(pl.multiple_of(r * ROWS, 8), ROWS)
        values = wide(t0[at, :], t1[at, :])
        plain[r] = values.astype(BF16)
        weighted[r] = (values * waves_ref[1:2, :]).astype(BF16)

    loop(MM, narrow_tables)

    def build_mix(g):
        real = weight_ref[2 * g]
        imag = weight_ref[2 * g + 1]
        mix[g, 0:128, 0:128] = real
        mix[g, 0:128, 128:256] = imag
        mix[g, 128:256, 0:128] = -imag
        mix[g, 128:256, 128:256] = real

    loop(2 * HB, build_mix)

    def fire_columns(j):
        fire_t[j] = fire_g[j].T[0:32]

    loop(JL, fire_columns)

    def analyse(c, k, hk, table, rows_of):
        first, count, height = PARTS[c]

        def one(i):
            low = mm_nn(table[i][:, 0:ROWS], rows_of(0, i))
            high = mm_nn(table[HB + i][:, 0:ROWS], rows_of(1, i))
            for p in range(2):
                lane = slice(p * 128, (p + 1) * 128)
                for ii in range(HB):
                    ll = low[ii * NS : (ii + 1) * NS, lane]
                    lh = low[(HB + ii) * NS : (HB + ii + 1) * NS, lane]
                    hh = high[(HB + ii) * NS : (HB + ii + 1) * NS, lane]
                    at = p * 10 * count + ii * count + i - first
                    made[pl.ds(at, NS, stride=height), :] = lh
                    made[pl.ds(at + 5 * count, NS, stride=height), :] = jnp.where(row16 >= me, ll, hh)
                    extra[pl.ds(p * 32 + i * HB + ii, NS, stride=64), :] = rounded(hh)

        loop(first + count, one, first)
        exchange(
            hsend[c].at[hk], hrecv[c].at[hk], pl.ds(0, height), k, lambda e: e * height
        )

    def first_rows(h, i):
        a = taken[pl.ds(i * 640 + h, ROWS, stride=4), :]
        b = taken[pl.ds(i * 640 + 2 + h, ROWS, stride=4), :]
        return wide(a, b).astype(BF16)

    def later_rows(h, i):
        a = taken[pl.ds(h * HB + i, ROWS, stride=2 * MM), :]
        b = taken[pl.ds(MM + h * HB + i, ROWS, stride=2 * MM), :]
        return wide(a, b).astype(BF16)

    def mix_degrees(c, hk_in, k_in, hk_out, k_out, backward):
        first, count, height = PARTS[c]
        n = count * NS
        at = pl.ds(0, height)
        arrived(hsend[c].at[hk_in], hrecv[c].at[hk_in], at, k_in, lambda s: s * height)
        product = mm_nt if backward else mm_nn
        from_low = (lax.broadcasted_iota(jnp.int32, (n, 256), 0) & 15) <= me
        for ii in range(HB):

            def gather(slot):
                pieces = []
                for i in range(count):
                    r = slot * 5 * count + ii * count + i
                    pieces.append(
                        wide(
                            taken[pl.ds(r, NS, stride=height), :],
                            taken[pl.ds(10 * count + r, NS, stride=height), :],
                        )
                    )
                return jnp.concatenate(pieces, axis=0)

            own = wide(
                extra[pl.ds(me * 64 + first * HB + ii, 8, stride=HB), :],
                extra[pl.ds(me * 64 + 32 + first * HB + ii, 8, stride=HB), :],
            )
            own = jnp.where(lax.broadcasted_iota(jnp.int32, (8, 256), 0) < count, own, 0.0)
            second = gather(1)
            rows = jnp.concatenate([gather(0), second, own, jnp.zeros((8, 256), F32)], axis=0)
            narrow = rows.astype(BF16)
            high = product(narrow, mix[HB + ii])
            low = product(second.astype(BF16), mix[ii])
            mixed_second = jnp.where(from_low, low, high[n : 2 * n])
            for p in range(2):
                lane = slice(p * 128, (p + 1) * 128)
                for i in range(count):
                    r = p * 10 * count + ii * count + i
                    piece = slice(i * NS, (i + 1) * NS)
                    made[pl.ds(r, NS, stride=height), :] = high[piece, lane]
                    made[pl.ds(r + 5 * count, NS, stride=height), :] = mixed_second[piece, lane]
                at_own = p * 32 + ii * count
                back[c][at_own : at_own + 8, :] = rounded(high[2 * n : 2 * n + 8, lane])
            if backward:
                grad_rows[c][ii] = narrow
            else:
                coef[c][ii] = narrow
        exchange(hsend[c].at[hk_out], hrecv[c].at[hk_out], at, k_out, lambda e: e * height)

    def weight_gradient(ii):
        grad_low = jnp.zeros((256, 256), F32)
        grad_high = jnp.zeros((256, 256), F32)
        for c, (_, count, _) in enumerate(PARTS):
            n = count * NS
            kept = coef[c][ii].astype(F32)
            others = grad_rows[c][ii]
            from_low = (lax.broadcasted_iota(jnp.int32, (n, 256), 0) & 15) <= me
            second = kept[n : 2 * n]
            kept_high = jnp.concatenate(
                [kept[0:n], jnp.where(from_low, 0.0, second), kept[2 * n : 2 * n + 16]], axis=0
            )
            kept_low = jnp.where(from_low, second, 0.0)
            grad_high = grad_high + mm_tn(kept_high.astype(BF16), others)
            grad_low = grad_low + mm_tn(kept_low.astype(BF16), others[n : 2 * n])
        for half, grad in ((0, grad_low), (1, grad_high)):
            at = pl.multiple_of((half * HB + ii) * 256, 256)
            spec[pl.ds(at, 128), :] = grad[0:128, 0:128] + grad[128:256, 128:256]
            spec[pl.ds(at + 128, 128), :] = grad[0:128, 128:256] - grad[128:256, 0:128]

    def synthesise(c, hk, k_in, table):
        first, count, height = PARTS[c]
        arrived(
            hsend[c].at[hk], hrecv[c].at[hk], pl.ds(0, height), k_in, lambda s: s * height
        )

        def one(i):
            def rows_of(slot, ii):
                r = slot * 5 * count + ii * count + i - first
                return wide(
                    taken[pl.ds(r, NS, stride=height), :],
                    taken[pl.ds(10 * count + r, NS, stride=height), :],
                )

            seconds = [rows_of(1, ii) for ii in range(HB)]
            firsts = [rows_of(0, ii) for ii in range(HB)]
            mine = lax.broadcasted_iota(jnp.int32, (NS, 256), 0) == me
            highs = []
            for ii in range(HB):
                r = ii * count + i - first
                own = wide(back[c][pl.ds(r, 1), :], back[c][pl.ds(32 + r, 1), :])
                highs.append(jnp.where(mine, jnp.broadcast_to(own, (NS, 256)), seconds[ii]))
            low = mm_tn(
                table[i][:, 0:ROWS], jnp.concatenate(seconds + firsts, axis=0).astype(BF16)
            )
            high = mm_tn(
                table[HB + i][:, 0:ROWS], jnp.concatenate(seconds + highs, axis=0).astype(BF16)
            )
            made[pl.ds(i, ROWS, stride=2 * MM), :] = low[:, 0:128]
            made[pl.ds(MM + i, ROWS, stride=2 * MM), :] = low[:, 128:256]
            made[pl.ds(HB + i, ROWS, stride=2 * MM), :] = high[:, 0:128]
            made[pl.ds(MM + HB + i, ROWS, stride=2 * MM), :] = high[:, 128:256]

        loop(first + count, one, first)

    def pair_rows(c):
        return pl.ds(pl.multiple_of(c * PAIR, 8), PAIR)

    def send_pair(fk, k, c):
        exchange(fsend.at[fk], frecv.at[fk], pair_rows(c), k + c, lambda e: e * FULL + c * PAIR)

    def take_pair(fk, k, c):
        arrived(fsend.at[fk], frecv.at[fk], pair_rows(c), k + c, lambda s: s * FULL + c * PAIR)

    def from_orders(j, table):
        pieces = [taken[pl.ds(j * (2 * MM) + r, NS, stride=FULL), :] for r in range(2 * MM)]
        return mm_nn(table[...], jnp.concatenate(pieces, axis=0).astype(BF16))

    for c, (first, count, _) in enumerate(PARTS):
        for i in range(first, first + count):
            at = pl.ds(i * PAIR, PAIR)
            if i == first:
                whole(fsend.at[0], frecv.at[0], first_at[c], c).wait_recv()

            def first_block(s):
                taken[pl.ds(pl.multiple_of(i * 640 + s * PAIR, 8), PAIR), :] = frecv[0, s, at, :].astype(F32)

            loop(NS, first_block)
        analyse(c, 2 + c, 0, weighted, first_rows)
    for c in range(2):
        mix_degrees(c, 0, 2 + c, 1, 4 + c, False)
    for c in range(2):
        synthesise(c, 1, 4 + c, plain)
    loop(HB, lambda c: send_pair(1, 6, c))

    small[...] = jnp.zeros((640, CHAN), F32)

    def middle_row(j):
        row = normed[j]
        inner = from_orders(j, synt_ref) + mm_nn(row, skip_ref[...])
        activated, inner_slope = gelu_parts(inner)
        second, factor = normalize(activated)
        narrow = second.astype(BF16)
        upper = mm_nn(narrow, up_ref[...])
        hidden, slope = gelu_parts(upper)
        incoming = cot_ref[j]
        grad_upper = (mm_nt(incoming, down_ref[...]) * slope).astype(BF16)
        grad_second = mm_nt(grad_upper, up_ref[...])
        small[384:640, :] += mm_tn(hidden.astype(BF16), incoming)
        grad_up = mm_tn(narrow, grad_upper)
        small[128:256, :] += grad_up[:, 0:128]
        small[256:384, :] += grad_up[:, 128:256]
        grad_inner = (normalize_grad(second, factor, grad_second) * inner_slope).astype(BF16)
        small[0:128, :] += mm_tn(row, grad_inner)
        inner_grad[j] = grad_inner
        spectrum = mm_nn(syn_ref[...], grad_inner)
        for r in range(2 * MM):
            made[pl.ds(j * (2 * MM) + r, NS, stride=FULL), :] = spectrum[r * NS : (r + 1) * NS]

    def middle_pair(c):
        take_pair(1, 6, c)
        loop(2, lambda t: middle_row(2 * c + t))
        send_pair(2, 11, c)

    loop(HB, middle_pair)

    def small_source(t):
        return small.at[pl.ds(pl.multiple_of(t * pr, 8), pr), :]

    spread("dp", nd, dp, 0, small_source, small_in, True)
    small_in[dp] = small[pl.ds(pl.multiple_of(dp * pr, 8), pr), :]

    loop(HB, lambda c: take_pair(2, 11, c))
    for c in range(2):
        analyse(c, 16 + c, 2, plain, later_rows)

    spread("dp", nd, dp, 0, small_source, small_in, False)
    piece1[...] = total(small_in, nd)

    def owner_copy(e, slot):
        return pltpu.make_async_remote_copy(
            src_ref=piece1.at[pl.ds(pl.multiple_of(e * og, 8), og)],
            dst_ref=own_in.at[slot],
            send_sem=dsend.at[1],
            recv_sem=drecv.at[1],
            device_id={"space": e},
            device_id_type=MESH,
        )

    def to_owner(e):
        @pl.when(e != me)
        def _():
            owner_copy(e, me).start()

    loop(OWNERS, to_owner)

    for c in range(2):
        mix_degrees(c, 2, 16 + c, 3, 18 + c, True)

    def owner_out(t, slot):
        return pltpu.make_async_remote_copy(
            src_ref=own_sum,
            dst_ref=piece2.at[slot],
            send_sem=dsend.at[2],
            recv_sem=drecv.at[2],
            device_id={"space": t},
            device_id_type=MESH,
        )

    @pl.when(me < OWNERS)
    def _():
        own_in[me] = piece1[pl.ds(pl.multiple_of(me * og, 8), og), :]
        gathered = pltpu.make_async_remote_copy(
            src_ref=own_in.at[pl.ds(0, NS - 1)],
            dst_ref=own_in.at[pl.ds(0, NS - 1)],
            send_sem=dsend.at[1],
            recv_sem=drecv.at[1],
            device_id={"space": lax.rem(me + 1, NS)},
            device_id_type=MESH,
        )
        gathered.wait_recv()
        own_sum[...] = total(own_in, NS)
        piece2[me] = own_sum[...]

        def tell(o):
            owner_out(lax.rem(me + o, NS), me).start()

        loop(NS, tell, 1)

    loop(HB, weight_gradient)

    def narrow_spec(t):
        spec_send[t] = spec[pl.ds(pl.multiple_of(t * sr, 16), sr), :].astype(BF16)

    loop(nd, narrow_spec)
    spread("dp", nd, dp, 3, lambda t: spec_send.at[t], spec_in, True)
    spec_in[dp] = spec_send[dp]

    for c in range(2):
        synthesise(c, 3, 18 + c, weighted)
    loop(HB, lambda c: send_pair(3, 20, c))

    def counted(ref, count, k):
        return pltpu.make_async_remote_copy(
            src_ref=ref.at[pl.ds(0, count)],
            dst_ref=ref.at[pl.ds(0, count)],
            send_sem=dsend.at[k],
            recv_sem=drecv.at[k],
            device_id={"space": lax.rem(me + 1, NS)},
            device_id_type=MESH,
        )

    @pl.when(me < OWNERS)
    def _():
        counted(own_in, OWNERS - 1, 1).wait_send()
        counted(piece2, OWNERS - 1, 2).wait_recv()
        counted(own_in, NS - 1, 2).wait_send()

    @pl.when(me >= OWNERS)
    def _():
        counted(own_in, OWNERS, 1).wait_send()
        counted(piece2, OWNERS, 2).wait_recv()

    spread("dp", nd, dp, 4, lambda t: piece2, small_all, True)
    small_all[dp] = piece2[...]

    spread("dp", nd, dp, 3, lambda t: spec_send.at[t], spec_in, False)
    spec_piece[...] = total(spec_in, nd).astype(BF16)
    spread("dp", nd, dp, 5, lambda t: spec_piece, spec_all, True)
    spec_all[dp] = spec_piece[...]

    for c, at in enumerate(first_at):
        whole(fsend.at[0], frecv.at[0], at, c).wait_send()
    for k, hk in ((2, 0), (4, 1), (16, 2), (18, 3)):
        for c, (_, _, height) in enumerate(PARTS):
            whole(hsend[c].at[hk], hrecv[c].at[hk], pl.ds(0, height), k + c).wait_send()
    for k, fk in ((6, 1), (11, 2)):
        loop(HB, lambda c: whole(fsend.at[fk], frecv.at[fk], pair_rows(c), k + c).wait_send())

    tab_mine[...] = jnp.zeros((32, CHAN), F32)

    def last_row(j):
        grad_normed = from_orders(j, anat_ref) + mm_nt(inner_grad[j], skip_ref[...])
        grad = cot_ref[j].astype(F32) + normalize_grad(unit[j], scale[j], grad_normed)
        field_out[j] = grad.astype(BF16)
        tab_mine[...] += mm_exact(fire_t[j], grad)

    def last_pair(c):
        take_pair(3, 20, c)
        loop(2, lambda t: last_row(2 * c + t))

    loop(HB, last_pair)
    tab_mine[0:8, :] = tab_mine[0:8, :] + tab_mine[8:16, :] + tab_mine[16:24, :]
    spread("space", NS, me, 6, lambda t: tab_mine.at[0:8], tab_space, True)
    tab_space[me] = tab_mine[0:8, :]

    loop(HB, lambda c: whole(fsend.at[3], frecv.at[3], pair_rows(c), 20 + c).wait_send())
    spread("dp", nd, dp, 4, lambda t: piece2, small_all, False)
    flat_small = [small_all[t, g] for t in range(nd) for g in range(OWNERS)]
    flat_small = jnp.concatenate(flat_small, axis=0)
    skip_out[...] = flat_small[0:128]
    up_out[:, 0:128] = flat_small[128:256]
    up_out[:, 128:256] = flat_small[256:384]
    down_out[...] = flat_small[384:640]
    spread("dp", nd, dp, 5, lambda t: spec_piece, spec_all, False)

    def copy_spec(t):
        spectral_out[pl.ds(pl.multiple_of(t * sr, 16), sr), :] = spec_all[t]

    loop(nd, copy_spec)

    spread("space", NS, me, 6, lambda t: tab_mine.at[0:8], tab_space, False)
    tab_sum[...] = total(tab_space, NS)
    spread("dp", nd, dp, 7, lambda t: tab_sum, tab_dp, True)
    tab_dp[dp] = tab_sum[...]
    spread("dp", nd, dp, 7, lambda t: tab_sum, tab_dp, False)
    table_out[...] = total(tab_dp, nd)


def shards(
    nd,
    state_field,
    cotangent,
    fire_cells,
    fire_kinds,
    fire_heat,
    forcing_table,
    spectral_weight,
    skip_weight,
    up_weight,
    down_weight,
):
    ana, anat, syn, synt, start, waves = (jnp.asarray(t) for t in constant_tables())
    pr, sr = 640 // nd, 2560 // nd
    operands = (
        state_field[0],
        cotangent[0],
        fire_cells,
        fire_kinds,
        fire_heat,
        forcing_table,
        spectral_weight.reshape(4 * HB, CHAN, CHAN),
        skip_weight,
        up_weight,
        down_weight,
        ana,
        anat,
        syn,
        synt,
        start,
        waves,
    )
    vmem = pl.BlockSpec(memory_space=pltpu.VMEM)
    out_shape = (
        jax.ShapeDtypeStruct((JL, NLON, CHAN), BF16),
        jax.ShapeDtypeStruct((2560, CHAN), BF16),
        jax.ShapeDtypeStruct((CHAN, CHAN), F32),
        jax.ShapeDtypeStruct((CHAN, HIDDEN), F32),
        jax.ShapeDtypeStruct((HIDDEN, CHAN), F32),
        jax.ShapeDtypeStruct((FORCE, CHAN), F32),
    )
    (_, ca, ha), (_, cb, hb) = PARTS
    scratch = [
        pltpu.VMEM((JL, NLON, CHAN), F32),
        pltpu.VMEM((JL, NLON, CHAN), F32),
        pltpu.VMEM((JL, NLON, CHAN), BF16),
        pltpu.VMEM((JL, NLON, CHAN), BF16),
        pltpu.VMEM((JL, NLON, CHAN), F32),
        pltpu.VMEM((JL, 32, NLON), F32),
        pltpu.VMEM((NS * FULL, CHAN), F32),
        pltpu.VMEM((NS * FULL, CHAN), F32),
        pltpu.VMEM((4, NS, FULL, CHAN), BF16),
        pltpu.VMEM((4, NS, FULL, CHAN), BF16),
        pltpu.VMEM((4, NS, ha, CHAN), BF16),
        pltpu.VMEM((4, NS, ha, CHAN), BF16),
        pltpu.VMEM((4, NS, hb, CHAN), BF16),
        pltpu.VMEM((4, NS, hb, CHAN), BF16),
        pltpu.VMEM((NS * 64 + 32, CHAN), F32),
        pltpu.VMEM((64, CHAN), F32),
        pltpu.VMEM((64, CHAN), F32),
        pltpu.VMEM((16 * ROWS, 128), F32),
        pltpu.VMEM((16 * ROWS, 128), F32),
        pltpu.VMEM((MM, ROWS, 256), BF16),
        pltpu.VMEM((MM, ROWS, 256), BF16),
        pltpu.VMEM((2 * HB, 256, 256), BF16),
        pltpu.VMEM((HB, 2 * NS * ca + 16, 256), BF16),
        pltpu.VMEM((HB, 2 * NS * cb + 16, 256), BF16),
        pltpu.VMEM((HB, 2 * NS * ca + 16, 256), BF16),
        pltpu.VMEM((HB, 2 * NS * cb + 16, 256), BF16),
        pltpu.VMEM((640, CHAN), F32),
        pltpu.VMEM((nd, pr, CHAN), F32),
        pltpu.VMEM((pr, CHAN), F32),
        pltpu.VMEM((NS, pr // OWNERS, CHAN), F32),
        pltpu.VMEM((pr // OWNERS, CHAN), F32),
        pltpu.VMEM((OWNERS, pr // OWNERS, CHAN), F32),
        pltpu.VMEM((nd, OWNERS, pr // OWNERS, CHAN), F32),
        pltpu.VMEM((2560, CHAN), F32),
        pltpu.VMEM((nd, sr, CHAN), BF16),
        pltpu.VMEM((nd, sr, CHAN), BF16),
        pltpu.VMEM((sr, CHAN), BF16),
        pltpu.VMEM((nd, sr, CHAN), BF16),
        pltpu.VMEM((32, CHAN), F32),
        pltpu.VMEM((NS, FORCE, CHAN), F32),
        pltpu.VMEM((FORCE, CHAN), F32),
        pltpu.VMEM((nd, FORCE, CHAN), F32),
        pltpu.SemaphoreType.DMA((25,)),
        pltpu.SemaphoreType.DMA((25,)),
        pltpu.SemaphoreType.DMA((8,)),
        pltpu.SemaphoreType.DMA((8,)),
    ]
    field, spectral, skip, up, down, table = pl.pallas_call(
        functools.partial(step_kernel, nd),
        out_shape=out_shape,
        in_specs=[vmem] * len(operands),
        out_specs=(vmem,) * len(out_shape),
        scratch_shapes=scratch,
        compiler_params=pltpu.CompilerParams(
            collective_id=0, has_side_effects=True, vmem_limit_bytes=60 << 20
        ),
        name="step",
    )(*operands)
    spectral = spectral.reshape(spectral_weight.shape).astype(F32)
    return (field[None], spectral, skip, up, down, table)


def solution(mesh):
    return jax.shard_map(
        functools.partial(shards, mesh.shape["dp"]),
        mesh=mesh,
        in_specs=(
            P("dp", "space", None, None),
            P("dp", "space", None, None),
            P("dp", None),
            P("dp", None),
            P("dp", None),
            P(),
            P(None, "space", None, None, None),
            P(),
            P(),
            P(),
        ),
        out_specs=(
            P("dp", "space", None, None),
            P(None, "space", None, None, None),
            P(),
            P(),
            P(),
            P(),
        ),
        check_vma=False,
    )
```

```python
import functools
import math

import jax
import jax.numpy as jnp
import ml_dtypes
import numpy as np
from jax import lax
from jax.experimental import pallas as pl
from jax.experimental.pallas import tpu as pltpu
from jax.sharding import PartitionSpec as P

ROWS = 160
NLON = 320
CHAN = 128
HIDDEN = 256
FORCE = 8
FIRES = 256
NS = 16
JL = 10
HB = 5
MM = 10
FULL = 200
PARTS = ((0, 2, 40), (2, 3, 64))
ROW_PARTS = ((0, 8), (80, 12))
OPERANDS = 16
OWNERS = 5
EPSILON = 1e-06
MESH = pl.DeviceIdType.MESH
F32 = jnp.float32
BF16 = jnp.bfloat16
ROOT = math.sqrt(2.0 / math.pi)
CUBIC = 0.044715


def constant_tables():
    device = np.arange(NS)
    low = 5 * device[None, :] + np.arange(HB)[:, None]
    orders = np.stack([low, ROWS - 1 - low])
    flat = orders.reshape(-1)
    angle = 2.0 * np.pi * ((flat[:, None] * np.arange(NLON)[None, :]) % NLON) / NLON
    cosine, sine = np.cos(angle), np.sin(angle)
    factor = np.where(flat == 0, 1.0, 2.0)[:, None]
    analysis = np.concatenate([cosine, -sine], axis=0) / NLON
    synthesis = np.concatenate([factor * cosine, -factor * sine], axis=0)
    theta = np.pi * (np.arange(ROWS) + 0.5) / ROWS
    start = np.zeros((NS, 16, 256))
    for d in range(NS):
        for r in range(MM):
            m = float(orders[r // HB, r % HB, d])
            log_start = (
                0.5 * math.log((2.0 * m + 1.0) / (4.0 * math.pi))
                + 0.5 * (math.lgamma(m + 0.5) - math.lgamma(m + 1.0))
                - 0.25 * math.log(math.pi)
            )
            start[d, r, :ROWS] = np.exp(log_start + m * np.log(np.sin(theta)))
    waves = np.zeros((8, 256))
    waves[0, :ROWS] = np.cos(theta)
    waves[1, :ROWS] = 2.0 * np.pi * np.pi / ROWS * np.sin(theta)
    narrow = lambda t: np.ascontiguousarray(t).astype(np.float32).astype(ml_dtypes.bfloat16)
    return (
        narrow(analysis),
        narrow(analysis.T),
        narrow(synthesis),
        narrow(synthesis.T),
        start.astype(np.float32),
        waves.astype(np.float32),
    )


def mm_nn(a, b):
    return lax.dot_general(a, b, (((1,), (0,)), ((), ())), preferred_element_type=F32)


def mm_nt(a, b):
    return lax.dot_general(a, b, (((1,), (1,)), ((), ())), preferred_element_type=F32)


def mm_tn(a, b):
    return lax.dot_general(a, b, (((0,), (0,)), ((), ())), preferred_element_type=F32)


def mm_exact(a, b):
    return lax.dot_general(
        a, b, (((1,), (0,)), ((), ())), preferred_element_type=F32, precision=lax.Precision.HIGHEST
    )


def mean(values):
    return jnp.sum(values, axis=-1, keepdims=True) * (1.0 / CHAN)


def normalize(values):
    centre = values - mean(values)
    scale = lax.rsqrt(mean(centre * centre) + EPSILON)
    return centre * scale, scale


def normalize_grad(unit, scale, grad):
    return scale * (grad - mean(grad) - unit * mean(grad * unit))


def gelu_parts(v):
    square = v * v
    t = jnp.tanh(ROOT * v * (1.0 + CUBIC * square))
    half = 0.5 * (1.0 + t)
    slope = half + 0.5 * v * (1.0 - t * t) * (ROOT * (1.0 + 3.0 * CUBIC * square))
    return v * half, slope


def wide(a, b):
    return jnp.concatenate([a, b], axis=-1)


def loop(count, body, start=0):
    def step(index, carry):
        body(index)
        return carry

    lax.fori_loop(start, count, step, 0)


def rounded(v):
    return v.astype(BF16).astype(F32)


def step_kernel(nd, *refs):
    outside, results = refs[:OPERANDS], refs[OPERANDS : OPERANDS + 6]
    inside, sems = refs[OPERANDS + 6 : 2 * OPERANDS + 6], refs[2 * OPERANDS + 6]
    copies = [
        pltpu.make_async_copy(outside[n], inside[n], sems.at[n]) for n in range(OPERANDS)
    ]
    for copy in copies:
        copy.start()

    def ready(first, last):
        for copy in copies[first:last]:
            copy.wait()

    step_body(nd, ready, *inside, *results, *refs[2 * OPERANDS + 7 :])


def step_body(
    nd,
    ready,
    x_ref,
    cells_row,
    kinds_row,
    heat_row,
    table_ref,
    ana_ref,
    start_ref,
    waves_ref,
    weight_ref,
    cot_ref,
    synt_ref,
    skip_ref,
    up_ref,
    down_ref,
    syn_ref,
    anat_ref,
    field_out,
    spectral_out,
    skip_out,
    up_out,
    down_out,
    table_out,
    unit,
    scale,
    normed,
    inner_grad,
    fire_g,
    fire_t,
    taken,
    made,
    fsend,
    frecv,
    hsend_a,
    hrecv_a,
    hsend_b,
    hrecv_b,
    extra,
    back_a,
    back_b,
    t0,
    t1,
    plain,
    weighted,
    mix,
    coef_a,
    coef_b,
    grad_a,
    grad_b,
    small,
    small_in,
    piece1,
    own_in,
    own_sum,
    piece2,
    small_all,
    spec,
    spec_send,
    spec_core,
    spec_mine,
    spec_in,
    spec_piece,
    spec_all,
    tab_mine,
    tab_space,
    tab_sum,
    tab_dp,
    ssem,
    rsem,
    dsend,
    drecv,
):
    me = lax.axis_index("space")
    dp = lax.axis_index("dp")
    pr = 640 // nd
    sr = 1280 // max(nd // 2, 1)
    og = pr // OWNERS
    hsend, hrecv = (hsend_a, hsend_b), (hrecv_a, hrecv_b)
    back, coef, grad_rows = (back_a, back_b), (coef_a, coef_b), (grad_a, grad_b)

    barrier = pltpu.get_barrier_semaphore()

    def greet_space(o):
        pl.semaphore_signal(barrier, 1, device_id={"space": lax.rem(me + o, NS)}, device_id_type=MESH)

    def greet_dp(o):
        pl.semaphore_signal(barrier, 1, device_id={"dp": lax.rem(dp + o, nd)}, device_id_type=MESH)

    loop(NS, greet_space, 1)
    if nd > 1:
        loop(nd, greet_dp, 1)

    def exchange(send, recv, at, k, source):
        count = at.size

        def one(o):
            e = lax.rem(me + o, NS)
            send[e, at, :] = made[pl.ds(pl.multiple_of(source(e), 8), count), :].astype(BF16)
            pltpu.make_async_remote_copy(
                src_ref=send.at[e, at],
                dst_ref=recv.at[me, at],
                send_sem=ssem.at[k],
                recv_sem=rsem.at[k],
                device_id={"space": e},
                device_id_type=MESH,
            ).start()

        loop(NS, one, 1)
        recv[me, at, :] = made[pl.ds(pl.multiple_of(source(me), 8), count), :].astype(BF16)

    def whole(send, recv, at, k):
        return pltpu.make_async_remote_copy(
            src_ref=send.at[pl.ds(0, NS - 1), at],
            dst_ref=recv.at[pl.ds(0, NS - 1), at],
            send_sem=ssem.at[k],
            recv_sem=rsem.at[k],
            device_id={"space": lax.rem(me + 1, NS)},
            device_id_type=MESH,
        )

    def arrived(send, recv, at, k, target):
        whole(send, recv, at, k).wait_recv()

        def one(s):
            taken[pl.ds(pl.multiple_of(target(s), 8), at.size), :] = recv[s, at, :].astype(F32)

        loop(NS, one)

    def spread(axis, count, mine, k, source_of, recv, start):
        if count == 1:
            return
        if not start:
            done = pltpu.make_async_remote_copy(
                src_ref=recv.at[pl.ds(0, count - 1)],
                dst_ref=recv.at[pl.ds(0, count - 1)],
                send_sem=dsend.at[k],
                recv_sem=drecv.at[k],
                device_id={axis: lax.rem(mine + 1, count)},
                device_id_type=MESH,
            )
            done.wait_recv()
            done.wait_send()
            return

        def one(o):
            t = lax.rem(mine + o, count)
            pltpu.make_async_remote_copy(
                src_ref=source_of(t),
                dst_ref=recv.at[mine],
                send_sem=dsend.at[k],
                recv_sem=drecv.at[k],
                device_id={axis: t},
                device_id_type=MESH,
            ).start()

        loop(count, one, 1)

    def total(recv, count):
        value = recv[0].astype(F32)
        for t in range(1, count):
            value = value + recv[t].astype(F32)
        return value

    ready(0, 6)

    def column(row):
        return jnp.broadcast_to(row.astype(F32), (128, FIRES)).T

    lanes = lax.broadcasted_iota(jnp.int32, (FIRES, 128), 1)
    heat = column(heat_row[...])
    heat0 = rounded(heat)
    heat1 = rounded(heat - heat0)
    heat2 = heat - heat0 - heat1
    parts = jnp.where(lanes < 8, heat0, jnp.where(lanes < 16, heat1, heat2))
    chosen = (column(kinds_row[...]) == (lanes & 7).astype(F32)) & (lanes < 24)
    heats = jnp.where(chosen, parts, 0.0).astype(BF16)
    table_wide = table_ref[...].astype(F32)
    table3 = jnp.concatenate(
        [table_wide, table_wide, table_wide, jnp.zeros((104, CHAN), F32)], axis=0
    )

    def field_row(j):
        base = (me * JL + j) * NLON
        cells = lax.broadcasted_iota(jnp.int32, (NLON, FIRES), 0) + base
        hot = jnp.where(cells == cells_row[...], 1.0, 0.0).astype(BF16)
        fires = mm_nn(hot, heats)
        fire_g[j] = fires
        value, factor = normalize(x_ref[j].astype(F32) + mm_exact(fires, table3))
        unit[j] = value
        scale[j] = jnp.broadcast_to(factor, (NLON, CHAN))
        narrow = value.astype(BF16)
        normed[j] = narrow
        to_orders(j, ana_ref, narrow)

    def to_orders(j, table, row):
        spectrum = mm_nn(table[...], row)
        for c, (first, count, _) in enumerate(PARTS):
            start, width = ROW_PARTS[c]
            for r in range(width):
                p, h, i = r // (2 * count), r // count % 2, first + r % count
                at = (p * MM + h * HB + i) * NS
                made[pl.ds(start + j * width + r, NS, stride=FULL), :] = spectrum[at : at + NS]

    def rows_at(c, pair=None):
        start, width = ROW_PARTS[c]
        if pair is None:
            return pl.ds(start, JL * width)
        return pl.ds(pl.multiple_of(start + pair * 2 * width, 8), 2 * width)

    def send_rows(fk, k, c, pair=None):
        at = rows_at(c, pair)
        exchange(fsend.at[fk], frecv.at[fk], at, k, lambda e: e * FULL + at.start)

    def rows_arrived(fk, k, c, pair=None):
        at = rows_at(c, pair)
        start, width = ROW_PARTS[c]
        skip = NS * start - start
        arrived(
            fsend.at[fk], frecv.at[fk], at, k, lambda s: skip + s * (JL * width) + at.start
        )

    def taken_at(c, j, r):
        start, width = ROW_PARTS[c]
        return NS * start + j * width + r

    loop(2, field_row)
    pl.semaphore_wait(barrier, (NS - 1) + (nd - 1))

    def field_pair(pair):
        send_rows(0, pair, 0, pair)
        loop(2, lambda t: field_row(2 * pair + 2 + t))

    loop(HB - 1, field_pair)
    send_rows(0, HB - 1, 0, HB - 1)
    send_rows(0, HB, 1)

    ready(6, OPERANDS)
    row16 = lax.broadcasted_iota(jnp.int32, (16, 128), 0)
    order = jnp.where(row16 >= HB, ROWS - 1 - 5 * me - (row16 - HB), 5 * me + row16).astype(F32)
    order2 = order * order
    cos0 = jnp.broadcast_to(waves_ref[0:1, 0:128], (16, 128))
    cos1 = jnp.broadcast_to(waves_ref[0:1, 128:256], (16, 128))

    def advance(l, carry):
        p0, p1, b0, b1 = carry
        lf = jnp.full((16, 128), l, jnp.int32).astype(F32)
        lower = lf - 1.0
        upward = jnp.sqrt(
            jnp.maximum(4.0 * lf * lf - 1.0, 1.0) / jnp.maximum(lf * lf - order2, 1.0)
        )
        downward = jnp.sqrt(
            jnp.maximum(lower * lower - order2, 0.0) / jnp.maximum(4.0 * lower * lower - 1.0, 1.0)
        )
        first = start_ref[me]
        at_start = lf == order
        above = lf > order
        c0 = jnp.where(
            at_start, first[:, 0:128], jnp.where(above, upward * (cos0 * p0 - downward * b0), 0.0)
        )
        c1 = jnp.where(
            at_start, first[:, 128:256], jnp.where(above, upward * (cos1 * p1 - downward * b1), 0.0)
        )
        upper_half = l // 80
        q = l + upper_half * (ROWS - 1 - 2 * l)
        place = (upper_half * HB + q % HB) * NS + q // HB
        t0[pl.ds(place, 16, stride=ROWS), :] = c0
        t1[pl.ds(place, 16, stride=ROWS), :] = c1
        return (c0, c1, p0, p1)

    blank = start_ref[me][:, 0:128] * 0.0
    lax.fori_loop(0, ROWS, advance, (blank, blank, blank, blank))

    def narrow_tables(r):
        at = pl.ds(pl.multiple_of(r * ROWS, 8), ROWS)
        values = wide(t0[at, :], t1[at, :])
        plain[r] = values.astype(BF16)
        weighted[r] = (values * waves_ref[1:2, :]).astype(BF16)

    loop(MM, narrow_tables)

    def build_mix(g):
        real = weight_ref[2 * g]
        imag = weight_ref[2 * g + 1]
        mix[g, 0:128, 0:128] = real
        mix[g, 0:128, 128:256] = imag
        mix[g, 128:256, 0:128] = -imag
        mix[g, 128:256, 128:256] = real

    loop(2 * HB, build_mix)

    def fire_columns(j):
        fire_t[j] = fire_g[j].T[0:32]

    loop(JL, fire_columns)

    def analyse(c, k, hk, table):
        first, count, height = PARTS[c]
        rows_of = rows_of_order(c)

        def one(i):
            low = mm_nn(table[i][:, 0:ROWS], rows_of(0, i))
            high = mm_nn(table[HB + i][:, 0:ROWS], rows_of(1, i))
            for p in range(2):
                lane = slice(p * 128, (p + 1) * 128)
                for ii in range(HB):
                    ll = low[ii * NS : (ii + 1) * NS, lane]
                    lh = low[(HB + ii) * NS : (HB + ii + 1) * NS, lane]
                    hh = high[(HB + ii) * NS : (HB + ii + 1) * NS, lane]
                    at = p * 10 * count + ii * count + i - first
                    made[pl.ds(at, NS, stride=height), :] = lh
                    made[pl.ds(at + 5 * count, NS, stride=height), :] = jnp.where(row16 >= me, ll, hh)
                    extra[pl.ds(p * 32 + i * HB + ii, NS, stride=64), :] = rounded(hh)

        loop(first + count, one, first)
        exchange(
            hsend[c].at[hk], hrecv[c].at[hk], pl.ds(0, height), k, lambda e: e * height
        )

    def rows_of_order(c):
        first, count, _ = PARTS[c]
        _, width = ROW_PARTS[c]

        def rows(h, i):
            at = taken_at(c, 0, h * count + i - first)
            return wide(
                taken[pl.ds(at, ROWS, stride=width), :],
                taken[pl.ds(at + 2 * count, ROWS, stride=width), :],
            ).astype(BF16)

        return rows

    def mix_degrees(c, hk_in, k_in, hk_out, k_out, backward):
        first, count, height = PARTS[c]
        n = count * NS
        at = pl.ds(0, height)
        arrived(hsend[c].at[hk_in], hrecv[c].at[hk_in], at, k_in, lambda s: s * height)
        product = mm_nt if backward else mm_nn
        from_low = (lax.broadcasted_iota(jnp.int32, (n, 256), 0) & 15) <= me
        for ii in range(HB):

            def gather(slot):
                pieces = []
                for i in range(count):
                    r = slot * 5 * count + ii * count + i
                    pieces.append(
                        wide(
                            taken[pl.ds(r, NS, stride=height), :],
                            taken[pl.ds(10 * count + r, NS, stride=height), :],
                        )
                    )
                return jnp.concatenate(pieces, axis=0)

            own = wide(
                extra[pl.ds(me * 64 + first * HB + ii, 8, stride=HB), :],
                extra[pl.ds(me * 64 + 32 + first * HB + ii, 8, stride=HB), :],
            )
            own = jnp.where(lax.broadcasted_iota(jnp.int32, (8, 256), 0) < count, own, 0.0)
            second = gather(1)
            rows = jnp.concatenate([gather(0), second, own, jnp.zeros((8, 256), F32)], axis=0)
            narrow = rows.astype(BF16)
            high = product(narrow, mix[HB + ii])
            low = product(second.astype(BF16), mix[ii])
            mixed_second = jnp.where(from_low, low, high[n : 2 * n])
            for p in range(2):
                lane = slice(p * 128, (p + 1) * 128)
                for i in range(count):
                    r = p * 10 * count + ii * count + i
                    piece = slice(i * NS, (i + 1) * NS)
                    made[pl.ds(r, NS, stride=height), :] = high[piece, lane]
                    made[pl.ds(r + 5 * count, NS, stride=height), :] = mixed_second[piece, lane]
                at_own = p * 32 + ii * count
                back[c][at_own : at_own + 8, :] = rounded(high[2 * n : 2 * n + 8, lane])
            if backward:
                grad_rows[c][ii] = narrow
            else:
                coef[c][ii] = narrow
        exchange(hsend[c].at[hk_out], hrecv[c].at[hk_out], at, k_out, lambda e: e * height)

    def weight_gradient(ii):
        grad_low = jnp.zeros((256, 256), F32)
        grad_high = jnp.zeros((256, 256), F32)
        for c, (_, count, _) in enumerate(PARTS):
            n = count * NS
            kept = coef[c][ii].astype(F32)
            others = grad_rows[c][ii]
            from_low = (lax.broadcasted_iota(jnp.int32, (n, 256), 0) & 15) <= me
            second = kept[n : 2 * n]
            kept_high = jnp.concatenate(
                [kept[0:n], jnp.where(from_low, 0.0, second), kept[2 * n : 2 * n + 16]], axis=0
            )
            kept_low = jnp.where(from_low, second, 0.0)
            grad_high = grad_high + mm_tn(kept_high.astype(BF16), others)
            grad_low = grad_low + mm_tn(kept_low.astype(BF16), others[n : 2 * n])
        for half, grad in ((0, grad_low), (1, grad_high)):
            at = pl.multiple_of((half * HB + ii) * 256, 256)
            spec[pl.ds(at, 128), :] = grad[0:128, 0:128] + grad[128:256, 128:256]
            spec[pl.ds(at + 128, 128), :] = grad[0:128, 128:256] - grad[128:256, 0:128]

    def synthesise(c, hk, k_in, table):
        first, count, height = PARTS[c]
        _, width = ROW_PARTS[c]
        arrived(
            hsend[c].at[hk], hrecv[c].at[hk], pl.ds(0, height), k_in, lambda s: s * height
        )

        def one(i):
            def rows_of(slot, ii):
                r = slot * 5 * count + ii * count + i - first
                return wide(
                    taken[pl.ds(r, NS, stride=height), :],
                    taken[pl.ds(10 * count + r, NS, stride=height), :],
                )

            seconds = [rows_of(1, ii) for ii in range(HB)]
            firsts = [rows_of(0, ii) for ii in range(HB)]
            mine = lax.broadcasted_iota(jnp.int32, (NS, 256), 0) == me
            highs = []
            for ii in range(HB):
                r = ii * count + i - first
                own = wide(back[c][pl.ds(r, 1), :], back[c][pl.ds(32 + r, 1), :])
                highs.append(jnp.where(mine, jnp.broadcast_to(own, (NS, 256)), seconds[ii]))
            low = mm_tn(
                table[i][:, 0:ROWS], jnp.concatenate(seconds + firsts, axis=0).astype(BF16)
            )
            high = mm_tn(
                table[HB + i][:, 0:ROWS], jnp.concatenate(seconds + highs, axis=0).astype(BF16)
            )
            for p in range(2):
                lane = slice(p * 128, (p + 1) * 128)
                at = taken_at(c, 0, p * 2 * count + i - first)
                made[pl.ds(at, ROWS, stride=width), :] = low[:, lane]
                made[pl.ds(at + count, ROWS, stride=width), :] = high[:, lane]

        loop(first + count, one, first)

    def send_back(fk, k, c, pair=None):
        at = rows_at(c, pair)
        start, width = ROW_PARTS[c]
        skip = NS * start - start
        exchange(
            fsend.at[fk], frecv.at[fk], at, k, lambda e: skip + e * (JL * width) + at.start
        )

    def from_orders(j, table):
        pieces = []
        for p in range(2):
            for h in range(2):
                for c, (_, count, _) in enumerate(PARTS):
                    _, width = ROW_PARTS[c]
                    for i in range(count):
                        at = taken_at(c, j, (p * 2 + h) * count + i)
                        pieces.append(taken[pl.ds(at, NS, stride=JL * width), :])
        return mm_nn(table[...], jnp.concatenate(pieces, axis=0).astype(BF16))

    def orders_arrived(fk, k, c):
        if c == 0:
            loop(HB, lambda pair: rows_arrived(fk, k + pair, 0, pair))
        else:
            rows_arrived(fk, k + HB, 1)

    for c in range(2):
        orders_arrived(0, 0, c)
        analyse(c, 6 + c, 0, weighted)
    for c in range(2):
        mix_degrees(c, 0, 6 + c, 1, 8 + c, False)
    synthesise(0, 1, 8, plain)
    send_back(1, 10, 0)
    synthesise(1, 1, 9, plain)
    loop(HB, lambda pair: send_back(1, 11 + pair, 1, pair))

    small[...] = jnp.zeros((640, CHAN), F32)

    def middle_row(j):
        row = normed[j]
        inner = from_orders(j, synt_ref) + mm_nn(row, skip_ref[...])
        activated, inner_slope = gelu_parts(inner)
        second, factor = normalize(activated)
        narrow = second.astype(BF16)
        upper = mm_nn(narrow, up_ref[...])
        hidden, slope = gelu_parts(upper)
        incoming = cot_ref[j]
        grad_upper = (mm_nt(incoming, down_ref[...]) * slope).astype(BF16)
        grad_second = mm_nt(grad_upper, up_ref[...])
        small[384:640, :] += mm_tn(hidden.astype(BF16), incoming)
        grad_up = mm_tn(narrow, grad_upper)
        small[128:256, :] += grad_up[:, 0:128]
        small[256:384, :] += grad_up[:, 128:256]
        grad_inner = (normalize_grad(second, factor, grad_second) * inner_slope).astype(BF16)
        small[0:128, :] += mm_tn(row, grad_inner)
        inner_grad[j] = grad_inner
        to_orders(j, syn_ref, grad_inner)

    rows_arrived(1, 10, 0)

    def middle_pair(pair):
        rows_arrived(1, 11 + pair, 1, pair)
        loop(2, lambda t: middle_row(2 * pair + t))
        send_rows(2, 16 + pair, 0, pair)

    loop(HB, middle_pair)
    send_rows(2, 16 + HB, 1)

    def small_source(t):
        return small.at[pl.ds(pl.multiple_of(t * pr, 8), pr), :]

    spread("dp", nd, dp, 0, small_source, small_in, True)
    small_in[dp] = small[pl.ds(pl.multiple_of(dp * pr, 8), pr), :]

    for c in range(2):
        orders_arrived(2, 16, c)
        analyse(c, 22 + c, 2, plain)

    spread("dp", nd, dp, 0, small_source, small_in, False)
    piece1[...] = total(small_in, nd)

    def owner_copy(e, slot):
        return pltpu.make_async_remote_copy(
            src_ref=piece1.at[pl.ds(pl.multiple_of(e * og, 8), og)],
            dst_ref=own_in.at[slot],
            send_sem=dsend.at[1],
            recv_sem=drecv.at[1],
            device_id={"space": e},
            device_id_type=MESH,
        )

    def to_owner(e):
        @pl.when(e != me)
        def _():
            owner_copy(e, me).start()

    loop(OWNERS, to_owner)

    for c in range(2):
        mix_degrees(c, 2, 22 + c, 3, 24 + c, True)

    def owner_out(t, slot):
        return pltpu.make_async_remote_copy(
            src_ref=own_sum,
            dst_ref=piece2.at[slot],
            send_sem=dsend.at[2],
            recv_sem=drecv.at[2],
            device_id={"space": t},
            device_id_type=MESH,
        )

    @pl.when(me < OWNERS)
    def _():
        own_in[me] = piece1[pl.ds(pl.multiple_of(me * og, 8), og), :]
        gathered = pltpu.make_async_remote_copy(
            src_ref=own_in.at[pl.ds(0, NS - 1)],
            dst_ref=own_in.at[pl.ds(0, NS - 1)],
            send_sem=dsend.at[1],
            recv_sem=drecv.at[1],
            device_id={"space": lax.rem(me + 1, NS)},
            device_id_type=MESH,
        )
        gathered.wait_recv()
        own_sum[...] = total(own_in, NS)
        piece2[me] = own_sum[...]

        def tell(o):
            owner_out(lax.rem(me + o, NS), me).start()

        loop(NS, tell, 1)

    loop(HB, weight_gradient)

    half = 1280
    nq = nd // 2
    core = lax.rem(dp, 2)
    chip = dp // 2

    def to_core(source, target, k):
        return pltpu.make_async_remote_copy(
            src_ref=source,
            dst_ref=target,
            send_sem=dsend.at[k],
            recv_sem=drecv.at[k],
            device_id={"dp": dp + 1 - 2 * core},
            device_id_type=MESH,
        )

    def to_chips(source_of, recv, k, start):
        if nq <= 1:
            return
        if not start:
            done = to_core(recv.at[pl.ds(0, nq - 1)], recv.at[pl.ds(0, nq - 1)], k)
            done.wait_recv()
            done.wait_send()
            return

        def one(o):
            t = lax.rem(chip + o, nq)
            pltpu.make_async_remote_copy(
                src_ref=source_of(t),
                dst_ref=recv.at[chip],
                send_sem=dsend.at[k],
                recv_sem=drecv.at[k],
                device_id={"dp": 2 * t + core},
                device_id_type=MESH,
            ).start()

        loop(nq, one, 1)

    def spec_first():
        if nd == 1:
            return
        other = pl.multiple_of((1 - core) * half, 128)
        spec_send[...] = spec[pl.ds(other, half), :].astype(BF16)
        to_core(spec_send, spec_core, 3).start()

    def spec_second():
        if nd == 1:
            return
        to_core(spec_send, spec_core, 3).wait_recv()
        mine = pl.multiple_of(core * half, 128)

        def add(t):
            at = pl.ds(pl.multiple_of(t * sr, 16), sr)
            both = spec[pl.ds(pl.multiple_of(mine + t * sr, 16), sr), :] + spec_core[at, :].astype(F32)
            spec_mine[t] = both.astype(BF16)

        loop(nq, add)
        to_chips(lambda t: spec_mine.at[t], spec_in, 5, True)
        spec_in[chip] = spec_mine[chip]

    def spec_third():
        if nd == 1:
            return
        to_core(spec_send, spec_core, 3).wait_send()
        to_chips(lambda t: spec_mine.at[t], spec_in, 5, False)
        spec_piece[...] = total(spec_in, nq).astype(BF16)
        to_chips(lambda t: spec_piece, spec_all.at[core], 6, True)
        spec_all[core, chip] = spec_piece[...]

    def spec_fourth():
        if nd == 1:
            return
        to_chips(lambda t: spec_piece, spec_all.at[core], 6, False)
        to_core(spec_all.at[core], spec_all.at[core], 7).start()

    def spec_fifth():
        if nd == 1:
            spectral_out[...] = spec[...]
            return
        to_core(spec_all.at[core], spec_all.at[1 - core], 7).wait()

        def widen(t):
            for c in range(2):
                at = pl.ds(pl.multiple_of(c * half + t * sr, 16), sr)
                spectral_out[at, :] = spec_all[c, t].astype(F32)

        loop(nq, widen)

    spec_first()
    synthesise(0, 3, 24, weighted)
    send_back(3, 26, 0)
    spec_second()
    synthesise(1, 3, 25, weighted)
    loop(HB, lambda pair: send_back(3, 27 + pair, 1, pair))

    def counted(ref, count, k):
        return pltpu.make_async_remote_copy(
            src_ref=ref.at[pl.ds(0, count)],
            dst_ref=ref.at[pl.ds(0, count)],
            send_sem=dsend.at[k],
            recv_sem=drecv.at[k],
            device_id={"space": lax.rem(me + 1, NS)},
            device_id_type=MESH,
        )

    @pl.when(me < OWNERS)
    def _():
        counted(own_in, OWNERS - 1, 1).wait_send()
        counted(piece2, OWNERS - 1, 2).wait_recv()
        counted(own_in, NS - 1, 2).wait_send()

    @pl.when(me >= OWNERS)
    def _():
        counted(own_in, OWNERS, 1).wait_send()
        counted(piece2, OWNERS, 2).wait_recv()

    spread("dp", nd, dp, 4, lambda t: piece2, small_all, True)
    small_all[dp] = piece2[...]

    spec_third()

    for k, fk in ((0, 0), (16, 2)):
        loop(HB, lambda pair: whole(fsend.at[fk], frecv.at[fk], rows_at(0, pair), k + pair).wait_send())
        whole(fsend.at[fk], frecv.at[fk], rows_at(1), k + HB).wait_send()
    for k, hk in ((6, 0), (8, 1), (22, 2), (24, 3)):
        for c, (_, _, height) in enumerate(PARTS):
            whole(hsend[c].at[hk], hrecv[c].at[hk], pl.ds(0, height), k + c).wait_send()

    def back_sent(k, fk):
        whole(fsend.at[fk], frecv.at[fk], rows_at(0), k).wait_send()
        loop(HB, lambda pair: whole(fsend.at[fk], frecv.at[fk], rows_at(1, pair), k + 1 + pair).wait_send())

    back_sent(10, 1)

    tab_mine[...] = jnp.zeros((32, CHAN), F32)

    def last_row(j):
        grad_normed = from_orders(j, anat_ref) + mm_nt(inner_grad[j], skip_ref[...])
        grad = cot_ref[j].astype(F32) + normalize_grad(unit[j], scale[j], grad_normed)
        field_out[j] = grad.astype(BF16)
        tab_mine[...] += mm_exact(fire_t[j], grad)

    rows_arrived(3, 26, 0)

    def last_pair(pair):
        rows_arrived(3, 27 + pair, 1, pair)
        loop(2, lambda t: last_row(2 * pair + t))

    loop(3, last_pair)
    spec_fourth()
    loop(HB, last_pair, 3)
    tab_mine[0:8, :] = tab_mine[0:8, :] + tab_mine[8:16, :] + tab_mine[16:24, :]
    spread("space", NS, me, 8, lambda t: tab_mine.at[0:8], tab_space, True)
    tab_space[me] = tab_mine[0:8, :]

    back_sent(26, 3)
    spread("dp", nd, dp, 4, lambda t: piece2, small_all, False)
    flat_small = [small_all[t, g] for t in range(nd) for g in range(OWNERS)]
    flat_small = jnp.concatenate(flat_small, axis=0)
    skip_out[...] = flat_small[0:128]
    up_out[:, 0:128] = flat_small[128:256]
    up_out[:, 128:256] = flat_small[256:384]
    down_out[...] = flat_small[384:640]
    spec_fifth()

    spread("space", NS, me, 8, lambda t: tab_mine.at[0:8], tab_space, False)
    tab_sum[...] = total(tab_space, NS)
    spread("dp", nd, dp, 9, lambda t: tab_sum, tab_dp, True)
    tab_dp[dp] = tab_sum[...]
    spread("dp", nd, dp, 9, lambda t: tab_sum, tab_dp, False)
    table_out[...] = total(tab_dp, nd)


def hand_over(*refs):
    sems = refs[-1]
    count = len(refs) // 2
    copies = [
        pltpu.make_async_copy(refs[n], refs[count + n], sems.at[n]) for n in range(count)
    ]
    for copy in copies:
        copy.start()
    for copy in copies:
        copy.wait()


def shards(
    nd,
    state_field,
    cotangent,
    fire_cells,
    fire_kinds,
    fire_heat,
    forcing_table,
    spectral_weight,
    skip_weight,
    up_weight,
    down_weight,
):
    ana, anat, syn, synt, start, waves = (jnp.asarray(t) for t in constant_tables())
    nq = max(nd // 2, 1)
    pr, sr = 640 // nd, 1280 // nq
    operands = (
        state_field[0],
        fire_cells,
        fire_kinds,
        fire_heat,
        forcing_table,
        ana,
        start,
        waves,
        spectral_weight.reshape(4 * HB, CHAN, CHAN),
        cotangent[0],
        synt,
        skip_weight,
        up_weight,
        down_weight,
        syn,
        anat,
    )
    vmem = pl.BlockSpec(memory_space=pltpu.VMEM)
    out_shape = (
        jax.ShapeDtypeStruct((JL, NLON, CHAN), BF16),
        jax.ShapeDtypeStruct((2560, CHAN), F32),
        jax.ShapeDtypeStruct((CHAN, CHAN), F32),
        jax.ShapeDtypeStruct((CHAN, HIDDEN), F32),
        jax.ShapeDtypeStruct((HIDDEN, CHAN), F32),
        jax.ShapeDtypeStruct((FORCE, CHAN), F32),
    )
    (_, ca, ha), (_, cb, hb) = PARTS
    outside = pl.BlockSpec(memory_space=pltpu.HBM)
    scratch = [pltpu.VMEM(v.shape, v.dtype) for v in operands]
    scratch += [
        pltpu.SemaphoreType.DMA((OPERANDS,)),
        pltpu.VMEM((JL, NLON, CHAN), F32),
        pltpu.VMEM((JL, NLON, CHAN), F32),
        pltpu.VMEM((JL, NLON, CHAN), BF16),
        pltpu.VMEM((JL, NLON, CHAN), BF16),
        pltpu.VMEM((JL, NLON, CHAN), F32),
        pltpu.VMEM((JL, 32, NLON), F32),
        pltpu.VMEM((NS * FULL, CHAN), F32),
        pltpu.VMEM((NS * FULL, CHAN), F32),
        pltpu.VMEM((4, NS, FULL, CHAN), BF16),
        pltpu.VMEM((4, NS, FULL, CHAN), BF16),
        pltpu.VMEM((4, NS, ha, CHAN), BF16),
        pltpu.VMEM((4, NS, ha, CHAN), BF16),
        pltpu.VMEM((4, NS, hb, CHAN), BF16),
        pltpu.VMEM((4, NS, hb, CHAN), BF16),
        pltpu.VMEM((NS * 64 + 32, CHAN), F32),
        pltpu.VMEM((64, CHAN), F32),
        pltpu.VMEM((64, CHAN), F32),
        pltpu.VMEM((16 * ROWS, 128), F32),
        pltpu.VMEM((16 * ROWS, 128), F32),
        pltpu.VMEM((MM, ROWS, 256), BF16),
        pltpu.VMEM((MM, ROWS, 256), BF16),
        pltpu.VMEM((2 * HB, 256, 256), BF16),
        pltpu.VMEM((HB, 2 * NS * ca + 16, 256), BF16),
        pltpu.VMEM((HB, 2 * NS * cb + 16, 256), BF16),
        pltpu.VMEM((HB, 2 * NS * ca + 16, 256), BF16),
        pltpu.VMEM((HB, 2 * NS * cb + 16, 256), BF16),
        pltpu.VMEM((640, CHAN), F32),
        pltpu.VMEM((nd, pr, CHAN), F32),
        pltpu.VMEM((pr, CHAN), F32),
        pltpu.VMEM((NS, pr // OWNERS, CHAN), F32),
        pltpu.VMEM((pr // OWNERS, CHAN), F32),
        pltpu.VMEM((OWNERS, pr // OWNERS, CHAN), F32),
        pltpu.VMEM((nd, OWNERS, pr // OWNERS, CHAN), F32),
        pltpu.VMEM((2560, CHAN), F32),
        pltpu.VMEM((1280, CHAN), BF16),
        pltpu.VMEM((1280, CHAN), BF16),
        pltpu.VMEM((nq, sr, CHAN), BF16),
        pltpu.VMEM((nq, sr, CHAN), BF16),
        pltpu.VMEM((sr, CHAN), BF16),
        pltpu.VMEM((2, nq, sr, CHAN), BF16),
        pltpu.VMEM((32, CHAN), F32),
        pltpu.VMEM((NS, FORCE, CHAN), F32),
        pltpu.VMEM((FORCE, CHAN), F32),
        pltpu.VMEM((nd, FORCE, CHAN), F32),
        pltpu.SemaphoreType.DMA((32,)),
        pltpu.SemaphoreType.DMA((32,)),
        pltpu.SemaphoreType.DMA((10,)),
        pltpu.SemaphoreType.DMA((10,)),
    ]
    results = pl.pallas_call(
        functools.partial(step_kernel, nd),
        out_shape=out_shape,
        in_specs=[outside] * len(operands),
        out_specs=(vmem,) * len(out_shape),
        scratch_shapes=scratch,
        compiler_params=pltpu.CompilerParams(
            collective_id=0, has_side_effects=True, vmem_limit_bytes=60 << 20
        ),
        name="step",
    )(*operands)
    hbm = pl.BlockSpec(memory_space=pl.ANY)
    field, spectral, skip, up, down, table = pl.pallas_call(
        hand_over,
        out_shape=out_shape,
        in_specs=[vmem] * len(out_shape),
        out_specs=(hbm,) * len(out_shape),
        scratch_shapes=[pltpu.SemaphoreType.DMA((len(out_shape),))],
        name="hand_over",
    )(*results)
    return (field[None], spectral.reshape(spectral_weight.shape), skip, up, down, table)


def solution(mesh):
    return jax.shard_map(
        functools.partial(shards, mesh.shape["dp"]),
        mesh=mesh,
        in_specs=(
            P("dp", "space", None, None),
            P("dp", "space", None, None),
            P("dp", None),
            P("dp", None),
            P("dp", None),
            P(),
            P(None, "space", None, None, None),
            P(),
            P(),
            P(),
        ),
        out_specs=(
            P("dp", "space", None, None),
            P(None, "space", None, None, None),
            P(),
            P(),
            P(),
            P(),
        ),
        check_vma=False,
    )
```

```python
import functools
import math

import jax
import jax.numpy as jnp
import ml_dtypes
import numpy as np
from jax import lax
from jax.experimental import pallas as pl
from jax.experimental.pallas import tpu as pltpu
from jax.sharding import PartitionSpec as P

ROWS = 160
NLON = 320
CHAN = 128
HIDDEN = 256
FORCE = 8
FIRES = 256
NS = 16
JL = 10
HB = 5
MM = 10
FULL = 200
PARTS = ((0, 2, 40), (2, 3, 64))
ROW_PARTS = ((0, 8), (80, 12))
OPERANDS = 16
FAR_FIRST = (4, 12, 5, 11, 3, 13, 6, 10, 2, 14, 7, 9, 1, 15, 8)
OWNERS = 5
EPSILON = 1e-06
MESH = pl.DeviceIdType.MESH
F32 = jnp.float32
BF16 = jnp.bfloat16
ROOT = math.sqrt(2.0 / math.pi)
CUBIC = 0.044715


def constant_tables():
    device = np.arange(NS)
    low = 5 * device[None, :] + np.arange(HB)[:, None]
    orders = np.stack([low, ROWS - 1 - low])
    flat = orders.reshape(-1)
    angle = 2.0 * np.pi * ((flat[:, None] * np.arange(NLON)[None, :]) % NLON) / NLON
    cosine, sine = np.cos(angle), np.sin(angle)
    factor = np.where(flat == 0, 1.0, 2.0)[:, None]
    analysis = np.concatenate([cosine, -sine], axis=0) / NLON
    synthesis = np.concatenate([factor * cosine, -factor * sine], axis=0)
    theta = np.pi * (np.arange(ROWS) + 0.5) / ROWS
    start = np.zeros((NS, 16, 256))
    for d in range(NS):
        for r in range(MM):
            m = float(orders[r // HB, r % HB, d])
            log_start = (
                0.5 * math.log((2.0 * m + 1.0) / (4.0 * math.pi))
                + 0.5 * (math.lgamma(m + 0.5) - math.lgamma(m + 1.0))
                - 0.25 * math.log(math.pi)
            )
            start[d, r, :ROWS] = np.exp(log_start + m * np.log(np.sin(theta)))
    waves = np.zeros((8, 256))
    waves[0, :ROWS] = np.cos(theta)
    waves[1, :ROWS] = 2.0 * np.pi * np.pi / ROWS * np.sin(theta)
    narrow = lambda t: np.ascontiguousarray(t).astype(np.float32).astype(ml_dtypes.bfloat16)
    return (
        narrow(analysis),
        narrow(analysis.T),
        narrow(synthesis),
        narrow(synthesis.T),
        start.astype(np.float32),
        waves.astype(np.float32),
    )


def mm_nn(a, b):
    return lax.dot_general(a, b, (((1,), (0,)), ((), ())), preferred_element_type=F32)


def mm_nt(a, b):
    return lax.dot_general(a, b, (((1,), (1,)), ((), ())), preferred_element_type=F32)


def mm_tn(a, b):
    return lax.dot_general(a, b, (((0,), (0,)), ((), ())), preferred_element_type=F32)


def mm_exact(a, b):
    return lax.dot_general(
        a, b, (((1,), (0,)), ((), ())), preferred_element_type=F32, precision=lax.Precision.HIGHEST
    )


def mean(values):
    return jnp.sum(values, axis=-1, keepdims=True) * (1.0 / CHAN)


def normalize(values):
    centre = values - mean(values)
    scale = lax.rsqrt(mean(centre * centre) + EPSILON)
    return centre * scale, scale


def normalize_grad(unit, scale, grad):
    return scale * (grad - mean(grad) - unit * mean(grad * unit))


def gelu_parts(v):
    square = v * v
    t = jnp.tanh(ROOT * v * (1.0 + CUBIC * square))
    half = 0.5 * (1.0 + t)
    slope = half + 0.5 * v * (1.0 - t * t) * (ROOT * (1.0 + 3.0 * CUBIC * square))
    return v * half, slope


def wide(a, b):
    return jnp.concatenate([a, b], axis=-1)


def loop(count, body, start=0):
    def step(index, carry):
        body(index)
        return carry

    lax.fori_loop(start, count, step, 0)


def rounded(v):
    return v.astype(BF16).astype(F32)


def step_kernel(nd, *refs):
    outside, results = refs[:OPERANDS], refs[OPERANDS : OPERANDS + 6]
    inside, sems = refs[OPERANDS + 6 : 2 * OPERANDS + 6], refs[2 * OPERANDS + 6]
    copies = [
        pltpu.make_async_copy(outside[n], inside[n], sems.at[n]) for n in range(OPERANDS)
    ]
    for copy in copies:
        copy.start()

    def ready(first, last):
        for copy in copies[first:last]:
            copy.wait()

    step_body(nd, ready, *inside, *results, *refs[2 * OPERANDS + 7 :])


def step_body(
    nd,
    ready,
    x_ref,
    cells_row,
    kinds_row,
    heat_row,
    table_ref,
    ana_ref,
    start_ref,
    waves_ref,
    weight_ref,
    cot_ref,
    synt_ref,
    skip_ref,
    up_ref,
    down_ref,
    syn_ref,
    anat_ref,
    field_out,
    spectral_out,
    skip_out,
    up_out,
    down_out,
    table_out,
    unit,
    scale,
    normed,
    inner_grad,
    fire_g,
    fire_t,
    taken,
    made,
    fsend,
    frecv,
    hsend_a,
    hrecv_a,
    hsend_b,
    hrecv_b,
    extra,
    back_a,
    back_b,
    t0,
    t1,
    plain,
    weighted,
    mix,
    coef_a,
    coef_b,
    grad_a,
    grad_b,
    small,
    small_in,
    piece1,
    own_in,
    own_sum,
    piece2,
    small_all,
    spec,
    spec_send,
    spec_core,
    spec_mine,
    spec_in,
    spec_piece,
    spec_all,
    tab_mine,
    tab_space,
    tab_sum,
    tab_dp,
    ssem,
    rsem,
    dsend,
    drecv,
):
    me = lax.axis_index("space")
    dp = lax.axis_index("dp")
    pr = 640 // nd
    sr = 1280 // max(nd // 2, 1)
    og = pr // OWNERS
    hsend, hrecv = (hsend_a, hsend_b), (hrecv_a, hrecv_b)
    back, coef, grad_rows = (back_a, back_b), (coef_a, coef_b), (grad_a, grad_b)

    barrier = pltpu.get_barrier_semaphore()

    def greet_space(o):
        pl.semaphore_signal(barrier, 1, device_id={"space": lax.rem(me + o, NS)}, device_id_type=MESH)

    def greet_dp(o):
        pl.semaphore_signal(barrier, 1, device_id={"dp": lax.rem(dp + o, nd)}, device_id_type=MESH)

    loop(NS, greet_space, 1)
    if nd > 1:
        loop(nd, greet_dp, 1)

    def exchange(send, recv, at, k, source):
        count = at.size
        for e in range(NS):
            send[e, at, :] = made[pl.ds(pl.multiple_of(source(e), 8), count), :].astype(BF16)
        for o in FAR_FIRST:
            e = lax.rem(me + o, NS)
            pltpu.make_async_remote_copy(
                src_ref=send.at[e, at],
                dst_ref=recv.at[me, at],
                send_sem=ssem.at[k],
                recv_sem=rsem.at[k],
                device_id={"space": e},
                device_id_type=MESH,
            ).start()
        recv[me, at, :] = send[me, at, :]

    def whole(send, recv, at, k):
        return pltpu.make_async_remote_copy(
            src_ref=send.at[pl.ds(0, NS - 1), at],
            dst_ref=recv.at[pl.ds(0, NS - 1), at],
            send_sem=ssem.at[k],
            recv_sem=rsem.at[k],
            device_id={"space": lax.rem(me + 1, NS)},
            device_id_type=MESH,
        )

    def arrived(send, recv, at, k, target):
        whole(send, recv, at, k).wait_recv()

        for s in range(NS):
            taken[pl.ds(pl.multiple_of(target(s), 8), at.size), :] = recv[s, at, :].astype(F32)

    def spread(axis, count, mine, k, source_of, recv, start):
        if count == 1:
            return
        if not start:
            done = pltpu.make_async_remote_copy(
                src_ref=recv.at[pl.ds(0, count - 1)],
                dst_ref=recv.at[pl.ds(0, count - 1)],
                send_sem=dsend.at[k],
                recv_sem=drecv.at[k],
                device_id={axis: lax.rem(mine + 1, count)},
                device_id_type=MESH,
            )
            done.wait_recv()
            done.wait_send()
            return

        def one(o):
            t = lax.rem(mine + o, count)
            pltpu.make_async_remote_copy(
                src_ref=source_of(t),
                dst_ref=recv.at[mine],
                send_sem=dsend.at[k],
                recv_sem=drecv.at[k],
                device_id={axis: t},
                device_id_type=MESH,
            ).start()

        loop(count, one, 1)

    def total(recv, count):
        value = recv[0].astype(F32)
        for t in range(1, count):
            value = value + recv[t].astype(F32)
        return value

    ready(0, 6)

    def column(row):
        return jnp.broadcast_to(row.astype(F32), (128, FIRES)).T

    lanes = lax.broadcasted_iota(jnp.int32, (FIRES, 128), 1)
    heat = column(heat_row[...])
    heat0 = rounded(heat)
    heat1 = rounded(heat - heat0)
    heat2 = heat - heat0 - heat1
    parts = jnp.where(lanes < 8, heat0, jnp.where(lanes < 16, heat1, heat2))
    chosen = (column(kinds_row[...]) == (lanes & 7).astype(F32)) & (lanes < 24)
    heats = jnp.where(chosen, parts, 0.0).astype(BF16)
    table_wide = table_ref[...].astype(F32)
    table3 = jnp.concatenate(
        [table_wide, table_wide, table_wide, jnp.zeros((104, CHAN), F32)], axis=0
    )

    def field_row(j):
        base = (me * JL + j) * NLON
        cells = lax.broadcasted_iota(jnp.int32, (NLON, FIRES), 0) + base
        hot = jnp.where(cells == cells_row[...], 1.0, 0.0).astype(BF16)
        fires = mm_nn(hot, heats)
        fire_g[j] = fires
        value, factor = normalize(x_ref[j].astype(F32) + mm_exact(fires, table3))
        unit[j] = value
        scale[j] = jnp.broadcast_to(factor, (NLON, CHAN))
        narrow = value.astype(BF16)
        normed[j] = narrow
        to_orders(j, ana_ref, narrow)

    def to_orders(j, table, row):
        spectrum = mm_nn(table[...], row)
        for c, (first, count, _) in enumerate(PARTS):
            start, width = ROW_PARTS[c]
            for r in range(width):
                p, h, i = r // (2 * count), r // count % 2, first + r % count
                at = (p * MM + h * HB + i) * NS
                made[pl.ds(start + j * width + r, NS, stride=FULL), :] = spectrum[at : at + NS]

    def rows_at(c, pair=None):
        start, width = ROW_PARTS[c]
        if pair is None:
            return pl.ds(start, JL * width)
        return pl.ds(pl.multiple_of(start + pair * 2 * width, 8), 2 * width)

    def send_rows(fk, k, c, pair=None):
        at = rows_at(c, pair)
        exchange(fsend.at[fk], frecv.at[fk], at, k, lambda e: e * FULL + at.start)

    def rows_arrived(fk, k, c, pair=None):
        at = rows_at(c, pair)
        start, width = ROW_PARTS[c]
        skip = NS * start - start
        arrived(
            fsend.at[fk], frecv.at[fk], at, k, lambda s: skip + s * (JL * width) + at.start
        )

    def taken_at(c, j, r):
        start, width = ROW_PARTS[c]
        return NS * start + j * width + r

    loop(2, field_row)
    pl.semaphore_wait(barrier, (NS - 1) + (nd - 1))

    def field_pair(pair):
        send_rows(0, pair, 0, pair)
        loop(2, lambda t: field_row(2 * pair + 2 + t))

    loop(HB - 1, field_pair)
    send_rows(0, HB - 1, 0, HB - 1)
    send_rows(0, HB, 1)

    ready(6, OPERANDS)
    row16 = lax.broadcasted_iota(jnp.int32, (16, 128), 0)
    order = jnp.where(row16 >= HB, ROWS - 1 - 5 * me - (row16 - HB), 5 * me + row16).astype(F32)
    order2 = order * order
    cos0 = jnp.broadcast_to(waves_ref[0:1, 0:128], (16, 128))
    cos1 = jnp.broadcast_to(waves_ref[0:1, 128:256], (16, 128))

    def advance(l, carry):
        p0, p1, b0, b1 = carry
        lf = jnp.full((16, 128), l, jnp.int32).astype(F32)
        lower = lf - 1.0
        upward = jnp.sqrt(
            jnp.maximum(4.0 * lf * lf - 1.0, 1.0) / jnp.maximum(lf * lf - order2, 1.0)
        )
        downward = jnp.sqrt(
            jnp.maximum(lower * lower - order2, 0.0) / jnp.maximum(4.0 * lower * lower - 1.0, 1.0)
        )
        first = start_ref[me]
        at_start = lf == order
        above = lf > order
        c0 = jnp.where(
            at_start, first[:, 0:128], jnp.where(above, upward * (cos0 * p0 - downward * b0), 0.0)
        )
        c1 = jnp.where(
            at_start, first[:, 128:256], jnp.where(above, upward * (cos1 * p1 - downward * b1), 0.0)
        )
        upper_half = l // 80
        q = l + upper_half * (ROWS - 1 - 2 * l)
        place = (upper_half * HB + q % HB) * NS + q // HB
        t0[pl.ds(place, 16, stride=ROWS), :] = c0
        t1[pl.ds(place, 16, stride=ROWS), :] = c1
        return (c0, c1, p0, p1)

    blank = start_ref[me][:, 0:128] * 0.0
    lax.fori_loop(0, ROWS, advance, (blank, blank, blank, blank))

    def narrow_tables(r):
        at = pl.ds(pl.multiple_of(r * ROWS, 8), ROWS)
        values = wide(t0[at, :], t1[at, :])
        plain[r] = values.astype(BF16)
        weighted[r] = (values * waves_ref[1:2, :]).astype(BF16)

    loop(MM, narrow_tables)

    def build_mix(g):
        real = weight_ref[2 * g]
        imag = weight_ref[2 * g + 1]
        mix[g, 0:128, 0:128] = real
        mix[g, 0:128, 128:256] = imag
        mix[g, 128:256, 0:128] = -imag
        mix[g, 128:256, 128:256] = real

    loop(2 * HB, build_mix)

    def fire_columns(j):
        fire_t[j] = fire_g[j].T[0:32]

    loop(JL, fire_columns)

    def analyse(c, k, hk, table):
        first, count, height = PARTS[c]
        rows_of = rows_of_order(c)

        def one(i):
            low = mm_nn(table[i][:, 0:ROWS], rows_of(0, i))
            high = mm_nn(table[HB + i][:, 0:ROWS], rows_of(1, i))
            for p in range(2):
                lane = slice(p * 128, (p + 1) * 128)
                for ii in range(HB):
                    ll = low[ii * NS : (ii + 1) * NS, lane]
                    lh = low[(HB + ii) * NS : (HB + ii + 1) * NS, lane]
                    hh = high[(HB + ii) * NS : (HB + ii + 1) * NS, lane]
                    at = p * 10 * count + ii * count + i - first
                    made[pl.ds(at, NS, stride=height), :] = lh
                    made[pl.ds(at + 5 * count, NS, stride=height), :] = jnp.where(row16 >= me, ll, hh)
                    extra[pl.ds(p * 32 + i * HB + ii, NS, stride=64), :] = rounded(hh)

        loop(first + count, one, first)
        exchange(
            hsend[c].at[hk], hrecv[c].at[hk], pl.ds(0, height), k, lambda e: e * height
        )

    def rows_of_order(c):
        first, count, _ = PARTS[c]
        _, width = ROW_PARTS[c]

        def rows(h, i):
            at = taken_at(c, 0, h * count + i - first)
            return wide(
                taken[pl.ds(at, ROWS, stride=width), :],
                taken[pl.ds(at + 2 * count, ROWS, stride=width), :],
            ).astype(BF16)

        return rows

    def mix_degrees(c, hk_in, k_in, hk_out, k_out, backward):
        first, count, height = PARTS[c]
        n = count * NS
        at = pl.ds(0, height)
        arrived(hsend[c].at[hk_in], hrecv[c].at[hk_in], at, k_in, lambda s: s * height)
        product = mm_nt if backward else mm_nn
        from_low = (lax.broadcasted_iota(jnp.int32, (n, 256), 0) & 15) <= me
        for ii in range(HB):

            def gather(slot):
                pieces = []
                for i in range(count):
                    r = slot * 5 * count + ii * count + i
                    pieces.append(
                        wide(
                            taken[pl.ds(r, NS, stride=height), :],
                            taken[pl.ds(10 * count + r, NS, stride=height), :],
                        )
                    )
                return jnp.concatenate(pieces, axis=0)

            own = wide(
                extra[pl.ds(me * 64 + first * HB + ii, 8, stride=HB), :],
                extra[pl.ds(me * 64 + 32 + first * HB + ii, 8, stride=HB), :],
            )
            own = jnp.where(lax.broadcasted_iota(jnp.int32, (8, 256), 0) < count, own, 0.0)
            second = gather(1)
            rows = jnp.concatenate([gather(0), second, own, jnp.zeros((8, 256), F32)], axis=0)
            narrow = rows.astype(BF16)
            high = product(narrow, mix[HB + ii])
            low = product(second.astype(BF16), mix[ii])
            mixed_second = jnp.where(from_low, low, high[n : 2 * n])
            for p in range(2):
                lane = slice(p * 128, (p + 1) * 128)
                for i in range(count):
                    r = p * 10 * count + ii * count + i
                    piece = slice(i * NS, (i + 1) * NS)
                    made[pl.ds(r, NS, stride=height), :] = high[piece, lane]
                    made[pl.ds(r + 5 * count, NS, stride=height), :] = mixed_second[piece, lane]
                at_own = p * 32 + ii * count
                back[c][at_own : at_own + 8, :] = rounded(high[2 * n : 2 * n + 8, lane])
            if backward:
                grad_rows[c][ii] = narrow
            else:
                coef[c][ii] = narrow
        exchange(hsend[c].at[hk_out], hrecv[c].at[hk_out], at, k_out, lambda e: e * height)

    def weight_gradient(ii):
        grad_low = jnp.zeros((256, 256), F32)
        grad_high = jnp.zeros((256, 256), F32)
        for c, (_, count, _) in enumerate(PARTS):
            n = count * NS
            kept = coef[c][ii].astype(F32)
            others = grad_rows[c][ii]
            from_low = (lax.broadcasted_iota(jnp.int32, (n, 256), 0) & 15) <= me
            second = kept[n : 2 * n]
            kept_high = jnp.concatenate(
                [kept[0:n], jnp.where(from_low, 0.0, second), kept[2 * n : 2 * n + 16]], axis=0
            )
            kept_low = jnp.where(from_low, second, 0.0)
            grad_high = grad_high + mm_tn(kept_high.astype(BF16), others)
            grad_low = grad_low + mm_tn(kept_low.astype(BF16), others[n : 2 * n])
        for half, grad in ((0, grad_low), (1, grad_high)):
            at = pl.multiple_of((half * HB + ii) * 256, 256)
            spec[pl.ds(at, 128), :] = grad[0:128, 0:128] + grad[128:256, 128:256]
            spec[pl.ds(at + 128, 128), :] = grad[0:128, 128:256] - grad[128:256, 0:128]

    def synthesise(c, hk, k_in, table):
        first, count, height = PARTS[c]
        _, width = ROW_PARTS[c]
        arrived(
            hsend[c].at[hk], hrecv[c].at[hk], pl.ds(0, height), k_in, lambda s: s * height
        )

        def one(i):
            def rows_of(slot, ii):
                r = slot * 5 * count + ii * count + i - first
                return wide(
                    taken[pl.ds(r, NS, stride=height), :],
                    taken[pl.ds(10 * count + r, NS, stride=height), :],
                )

            seconds = [rows_of(1, ii) for ii in range(HB)]
            firsts = [rows_of(0, ii) for ii in range(HB)]
            mine = lax.broadcasted_iota(jnp.int32, (NS, 256), 0) == me
            highs = []
            for ii in range(HB):
                r = ii * count + i - first
                own = wide(back[c][pl.ds(r, 1), :], back[c][pl.ds(32 + r, 1), :])
                highs.append(jnp.where(mine, jnp.broadcast_to(own, (NS, 256)), seconds[ii]))
            low = mm_tn(
                table[i][:, 0:ROWS], jnp.concatenate(seconds + firsts, axis=0).astype(BF16)
            )
            high = mm_tn(
                table[HB + i][:, 0:ROWS], jnp.concatenate(seconds + highs, axis=0).astype(BF16)
            )
            for p in range(2):
                lane = slice(p * 128, (p + 1) * 128)
                at = taken_at(c, 0, p * 2 * count + i - first)
                made[pl.ds(at, ROWS, stride=width), :] = low[:, lane]
                made[pl.ds(at + count, ROWS, stride=width), :] = high[:, lane]

        loop(first + count, one, first)

    def send_back(fk, k, c, pair=None):
        at = rows_at(c, pair)
        start, width = ROW_PARTS[c]
        skip = NS * start - start
        exchange(
            fsend.at[fk], frecv.at[fk], at, k, lambda e: skip + e * (JL * width) + at.start
        )

    def from_orders(j, table):
        pieces = []
        for p in range(2):
            for h in range(2):
                for c, (_, count, _) in enumerate(PARTS):
                    _, width = ROW_PARTS[c]
                    for i in range(count):
                        at = taken_at(c, j, (p * 2 + h) * count + i)
                        pieces.append(taken[pl.ds(at, NS, stride=JL * width), :])
        return mm_nn(table[...], jnp.concatenate(pieces, axis=0).astype(BF16))

    def orders_arrived(fk, k, c):
        if c == 0:
            loop(HB, lambda pair: rows_arrived(fk, k + pair, 0, pair))
        else:
            rows_arrived(fk, k + HB, 1)

    for c in range(2):
        orders_arrived(0, 0, c)
        analyse(c, 6 + c, 0, weighted)
    for c in range(2):
        mix_degrees(c, 0, 6 + c, 1, 8 + c, False)
    synthesise(0, 1, 8, plain)
    send_back(1, 10, 0)
    synthesise(1, 1, 9, plain)
    loop(HB, lambda pair: send_back(1, 11 + pair, 1, pair))

    small[...] = jnp.zeros((640, CHAN), F32)

    def middle_row(j):
        row = normed[j]
        inner = from_orders(j, synt_ref) + mm_nn(row, skip_ref[...])
        activated, inner_slope = gelu_parts(inner)
        second, factor = normalize(activated)
        narrow = second.astype(BF16)
        upper = mm_nn(narrow, up_ref[...])
        hidden, slope = gelu_parts(upper)
        incoming = cot_ref[j]
        grad_upper = (mm_nt(incoming, down_ref[...]) * slope).astype(BF16)
        grad_second = mm_nt(grad_upper, up_ref[...])
        small[384:640, :] += mm_tn(hidden.astype(BF16), incoming)
        grad_up = mm_tn(narrow, grad_upper)
        small[128:256, :] += grad_up[:, 0:128]
        small[256:384, :] += grad_up[:, 128:256]
        grad_inner = (normalize_grad(second, factor, grad_second) * inner_slope).astype(BF16)
        small[0:128, :] += mm_tn(row, grad_inner)
        inner_grad[j] = grad_inner
        to_orders(j, syn_ref, grad_inner)

    rows_arrived(1, 10, 0)

    def middle_pair(pair):
        rows_arrived(1, 11 + pair, 1, pair)
        loop(2, lambda t: middle_row(2 * pair + t))
        send_rows(2, 16 + pair, 0, pair)

    loop(HB, middle_pair)
    send_rows(2, 16 + HB, 1)

    def small_source(t):
        return small.at[pl.ds(pl.multiple_of(t * pr, 8), pr), :]

    spread("dp", nd, dp, 0, small_source, small_in, True)
    small_in[dp] = small[pl.ds(pl.multiple_of(dp * pr, 8), pr), :]

    for c in range(2):
        orders_arrived(2, 16, c)
        analyse(c, 22 + c, 2, plain)

    spread("dp", nd, dp, 0, small_source, small_in, False)
    piece1[...] = total(small_in, nd)

    def owner_copy(e, slot):
        return pltpu.make_async_remote_copy(
            src_ref=piece1.at[pl.ds(pl.multiple_of(e * og, 8), og)],
            dst_ref=own_in.at[slot],
            send_sem=dsend.at[1],
            recv_sem=drecv.at[1],
            device_id={"space": e},
            device_id_type=MESH,
        )

    def to_owner(e):
        @pl.when(e != me)
        def _():
            owner_copy(e, me).start()

    loop(OWNERS, to_owner)

    for c in range(2):
        mix_degrees(c, 2, 22 + c, 3, 24 + c, True)

    def owner_out(t, slot):
        return pltpu.make_async_remote_copy(
            src_ref=own_sum,
            dst_ref=piece2.at[slot],
            send_sem=dsend.at[2],
            recv_sem=drecv.at[2],
            device_id={"space": t},
            device_id_type=MESH,
        )

    @pl.when(me < OWNERS)
    def _():
        own_in[me] = piece1[pl.ds(pl.multiple_of(me * og, 8), og), :]
        gathered = pltpu.make_async_remote_copy(
            src_ref=own_in.at[pl.ds(0, NS - 1)],
            dst_ref=own_in.at[pl.ds(0, NS - 1)],
            send_sem=dsend.at[1],
            recv_sem=drecv.at[1],
            device_id={"space": lax.rem(me + 1, NS)},
            device_id_type=MESH,
        )
        gathered.wait_recv()
        own_sum[...] = total(own_in, NS)
        piece2[me] = own_sum[...]

        def tell(o):
            owner_out(lax.rem(me + o, NS), me).start()

        loop(NS, tell, 1)

    loop(HB, weight_gradient)

    half = 1280
    nq = nd // 2
    core = lax.rem(dp, 2)
    chip = dp // 2

    def to_core(source, target, k):
        return pltpu.make_async_remote_copy(
            src_ref=source,
            dst_ref=target,
            send_sem=dsend.at[k],
            recv_sem=drecv.at[k],
            device_id={"dp": dp + 1 - 2 * core},
            device_id_type=MESH,
        )

    def to_chips(source_of, recv, k, start):
        if nq <= 1:
            return
        if not start:
            done = to_core(recv.at[pl.ds(0, nq - 1)], recv.at[pl.ds(0, nq - 1)], k)
            done.wait_recv()
            done.wait_send()
            return

        def one(o):
            t = lax.rem(chip + o, nq)
            pltpu.make_async_remote_copy(
                src_ref=source_of(t),
                dst_ref=recv.at[chip],
                send_sem=dsend.at[k],
                recv_sem=drecv.at[k],
                device_id={"dp": 2 * t + core},
                device_id_type=MESH,
            ).start()

        loop(nq, one, 1)

    def spec_first():
        if nd == 1:
            return
        other = pl.multiple_of((1 - core) * half, 128)
        spec_send[...] = spec[pl.ds(other, half), :].astype(BF16)
        to_core(spec_send, spec_core, 3).start()

    def spec_second():
        if nd == 1:
            return
        to_core(spec_send, spec_core, 3).wait_recv()
        mine = pl.multiple_of(core * half, 128)

        def add(t):
            at = pl.ds(pl.multiple_of(t * sr, 16), sr)
            both = spec[pl.ds(pl.multiple_of(mine + t * sr, 16), sr), :] + spec_core[at, :].astype(F32)
            spec_mine[t] = both.astype(BF16)

        loop(nq, add)
        to_chips(lambda t: spec_mine.at[t], spec_in, 5, True)
        spec_in[chip] = spec_mine[chip]

    def spec_third():
        if nd == 1:
            return
        to_core(spec_send, spec_core, 3).wait_send()
        to_chips(lambda t: spec_mine.at[t], spec_in, 5, False)
        spec_piece[...] = total(spec_in, nq).astype(BF16)
        to_chips(lambda t: spec_piece, spec_all.at[core], 6, True)
        spec_all[core, chip] = spec_piece[...]

    def spec_fourth():
        if nd == 1:
            return
        to_chips(lambda t: spec_piece, spec_all.at[core], 6, False)
        to_core(spec_all.at[core], spec_all.at[core], 7).start()

    def spec_fifth():
        if nd == 1:
            spectral_out[...] = spec[...]
            return
        to_core(spec_all.at[core], spec_all.at[1 - core], 7).wait()

        def widen(t):
            for c in range(2):
                at = pl.ds(pl.multiple_of(c * half + t * sr, 16), sr)
                spectral_out[at, :] = spec_all[c, t].astype(F32)

        loop(nq, widen)

    spec_first()
    synthesise(0, 3, 24, weighted)
    send_back(3, 26, 0)
    spec_second()
    synthesise(1, 3, 25, weighted)
    loop(HB, lambda pair: send_back(3, 27 + pair, 1, pair))

    def counted(ref, count, k):
        return pltpu.make_async_remote_copy(
            src_ref=ref.at[pl.ds(0, count)],
            dst_ref=ref.at[pl.ds(0, count)],
            send_sem=dsend.at[k],
            recv_sem=drecv.at[k],
            device_id={"space": lax.rem(me + 1, NS)},
            device_id_type=MESH,
        )

    @pl.when(me < OWNERS)
    def _():
        counted(own_in, OWNERS - 1, 1).wait_send()
        counted(piece2, OWNERS - 1, 2).wait_recv()
        counted(own_in, NS - 1, 2).wait_send()

    @pl.when(me >= OWNERS)
    def _():
        counted(own_in, OWNERS, 1).wait_send()
        counted(piece2, OWNERS, 2).wait_recv()

    spread("dp", nd, dp, 4, lambda t: piece2, small_all, True)
    small_all[dp] = piece2[...]

    spec_third()

    for k, fk in ((0, 0), (16, 2)):
        loop(HB, lambda pair: whole(fsend.at[fk], frecv.at[fk], rows_at(0, pair), k + pair).wait_send())
        whole(fsend.at[fk], frecv.at[fk], rows_at(1), k + HB).wait_send()
    for k, hk in ((6, 0), (8, 1), (22, 2), (24, 3)):
        for c, (_, _, height) in enumerate(PARTS):
            whole(hsend[c].at[hk], hrecv[c].at[hk], pl.ds(0, height), k + c).wait_send()

    def back_sent(k, fk):
        whole(fsend.at[fk], frecv.at[fk], rows_at(0), k).wait_send()
        loop(HB, lambda pair: whole(fsend.at[fk], frecv.at[fk], rows_at(1, pair), k + 1 + pair).wait_send())

    back_sent(10, 1)

    tab_mine[...] = jnp.zeros((32, CHAN), F32)

    def last_row(j):
        grad_normed = from_orders(j, anat_ref) + mm_nt(inner_grad[j], skip_ref[...])
        grad = cot_ref[j].astype(F32) + normalize_grad(unit[j], scale[j], grad_normed)
        field_out[j] = grad.astype(BF16)
        tab_mine[...] += mm_exact(fire_t[j], grad)

    rows_arrived(3, 26, 0)

    def last_pair(pair):
        rows_arrived(3, 27 + pair, 1, pair)
        loop(2, lambda t: last_row(2 * pair + t))

    loop(3, last_pair)
    spec_fourth()
    loop(HB, last_pair, 3)
    tab_mine[0:8, :] = tab_mine[0:8, :] + tab_mine[8:16, :] + tab_mine[16:24, :]
    spread("space", NS, me, 8, lambda t: tab_mine.at[0:8], tab_space, True)
    tab_space[me] = tab_mine[0:8, :]

    back_sent(26, 3)
    spread("dp", nd, dp, 4, lambda t: piece2, small_all, False)
    flat_small = [small_all[t, g] for t in range(nd) for g in range(OWNERS)]
    flat_small = jnp.concatenate(flat_small, axis=0)
    skip_out[...] = flat_small[0:128]
    up_out[:, 0:128] = flat_small[128:256]
    up_out[:, 128:256] = flat_small[256:384]
    down_out[...] = flat_small[384:640]
    spec_fifth()

    spread("space", NS, me, 8, lambda t: tab_mine.at[0:8], tab_space, False)
    tab_sum[...] = total(tab_space, NS)
    spread("dp", nd, dp, 9, lambda t: tab_sum, tab_dp, True)
    tab_dp[dp] = tab_sum[...]
    spread("dp", nd, dp, 9, lambda t: tab_sum, tab_dp, False)
    table_out[...] = total(tab_dp, nd)


def hand_over(*refs):
    sems = refs[-1]
    count = len(refs) // 2
    copies = [
        pltpu.make_async_copy(refs[n], refs[count + n], sems.at[n]) for n in range(count)
    ]
    for copy in copies:
        copy.start()
    for copy in copies:
        copy.wait()


def shards(
    nd,
    state_field,
    cotangent,
    fire_cells,
    fire_kinds,
    fire_heat,
    forcing_table,
    spectral_weight,
    skip_weight,
    up_weight,
    down_weight,
):
    ana, anat, syn, synt, start, waves = (jnp.asarray(t) for t in constant_tables())
    nq = max(nd // 2, 1)
    pr, sr = 640 // nd, 1280 // nq
    operands = (
        state_field[0],
        fire_cells,
        fire_kinds,
        fire_heat,
        forcing_table,
        ana,
        start,
        waves,
        spectral_weight.reshape(4 * HB, CHAN, CHAN),
        cotangent[0],
        synt,
        skip_weight,
        up_weight,
        down_weight,
        syn,
        anat,
    )
    vmem = pl.BlockSpec(memory_space=pltpu.VMEM)
    out_shape = (
        jax.ShapeDtypeStruct((JL, NLON, CHAN), BF16),
        jax.ShapeDtypeStruct((2560, CHAN), F32),
        jax.ShapeDtypeStruct((CHAN, CHAN), F32),
        jax.ShapeDtypeStruct((CHAN, HIDDEN), F32),
        jax.ShapeDtypeStruct((HIDDEN, CHAN), F32),
        jax.ShapeDtypeStruct((FORCE, CHAN), F32),
    )
    (_, ca, ha), (_, cb, hb) = PARTS
    outside = pl.BlockSpec(memory_space=pltpu.HBM)
    scratch = [pltpu.VMEM(v.shape, v.dtype) for v in operands]
    scratch += [
        pltpu.SemaphoreType.DMA((OPERANDS,)),
        pltpu.VMEM((JL, NLON, CHAN), F32),
        pltpu.VMEM((JL, NLON, CHAN), F32),
        pltpu.VMEM((JL, NLON, CHAN), BF16),
        pltpu.VMEM((JL, NLON, CHAN), BF16),
        pltpu.VMEM((JL, NLON, CHAN), F32),
        pltpu.VMEM((JL, 32, NLON), F32),
        pltpu.VMEM((NS * FULL, CHAN), F32),
        pltpu.VMEM((NS * FULL, CHAN), F32),
        pltpu.VMEM((4, NS, FULL, CHAN), BF16),
        pltpu.VMEM((4, NS, FULL, CHAN), BF16),
        pltpu.VMEM((4, NS, ha, CHAN), BF16),
        pltpu.VMEM((4, NS, ha, CHAN), BF16),
        pltpu.VMEM((4, NS, hb, CHAN), BF16),
        pltpu.VMEM((4, NS, hb, CHAN), BF16),
        pltpu.VMEM((NS * 64 + 32, CHAN), F32),
        pltpu.VMEM((64, CHAN), F32),
        pltpu.VMEM((64, CHAN), F32),
        pltpu.VMEM((16 * ROWS, 128), F32),
        pltpu.VMEM((16 * ROWS, 128), F32),
        pltpu.VMEM((MM, ROWS, 256), BF16),
        pltpu.VMEM((MM, ROWS, 256), BF16),
        pltpu.VMEM((2 * HB, 256, 256), BF16),
        pltpu.VMEM((HB, 2 * NS * ca + 16, 256), BF16),
        pltpu.VMEM((HB, 2 * NS * cb + 16, 256), BF16),
        pltpu.VMEM((HB, 2 * NS * ca + 16, 256), BF16),
        pltpu.VMEM((HB, 2 * NS * cb + 16, 256), BF16),
        pltpu.VMEM((640, CHAN), F32),
        pltpu.VMEM((nd, pr, CHAN), F32),
        pltpu.VMEM((pr, CHAN), F32),
        pltpu.VMEM((NS, pr // OWNERS, CHAN), F32),
        pltpu.VMEM((pr // OWNERS, CHAN), F32),
        pltpu.VMEM((OWNERS, pr // OWNERS, CHAN), F32),
        pltpu.VMEM((nd, OWNERS, pr // OWNERS, CHAN), F32),
        pltpu.VMEM((2560, CHAN), F32),
        pltpu.VMEM((1280, CHAN), BF16),
        pltpu.VMEM((1280, CHAN), BF16),
        pltpu.VMEM((nq, sr, CHAN), BF16),
        pltpu.VMEM((nq, sr, CHAN), BF16),
        pltpu.VMEM((sr, CHAN), BF16),
        pltpu.VMEM((2, nq, sr, CHAN), BF16),
        pltpu.VMEM((32, CHAN), F32),
        pltpu.VMEM((NS, FORCE, CHAN), F32),
        pltpu.VMEM((FORCE, CHAN), F32),
        pltpu.VMEM((nd, FORCE, CHAN), F32),
        pltpu.SemaphoreType.DMA((32,)),
        pltpu.SemaphoreType.DMA((32,)),
        pltpu.SemaphoreType.DMA((10,)),
        pltpu.SemaphoreType.DMA((10,)),
    ]
    results = pl.pallas_call(
        functools.partial(step_kernel, nd),
        out_shape=out_shape,
        in_specs=[outside] * len(operands),
        out_specs=(vmem,) * len(out_shape),
        scratch_shapes=scratch,
        compiler_params=pltpu.CompilerParams(
            collective_id=0, has_side_effects=True, vmem_limit_bytes=60 << 20
        ),
        name="step",
    )(*operands)
    hbm = pl.BlockSpec(memory_space=pl.ANY)
    field, spectral, skip, up, down, table = pl.pallas_call(
        hand_over,
        out_shape=out_shape,
        in_specs=[vmem] * len(out_shape),
        out_specs=(hbm,) * len(out_shape),
        scratch_shapes=[pltpu.SemaphoreType.DMA((len(out_shape),))],
        name="hand_over",
    )(*results)
    return (field[None], spectral.reshape(spectral_weight.shape), skip, up, down, table)


def solution(mesh):
    return jax.shard_map(
        functools.partial(shards, mesh.shape["dp"]),
        mesh=mesh,
        in_specs=(
            P("dp", "space", None, None),
            P("dp", "space", None, None),
            P("dp", None),
            P("dp", None),
            P("dp", None),
            P(),
            P(None, "space", None, None, None),
            P(),
            P(),
            P(),
        ),
        out_specs=(
            P("dp", "space", None, None),
            P(None, "space", None, None, None),
            P(),
            P(),
            P(),
            P(),
        ),
        check_vma=False,
    )
```

```python
import functools
import math

import jax
import jax.numpy as jnp
import ml_dtypes
import numpy as np
from jax import lax
from jax.experimental import pallas as pl
from jax.experimental.pallas import tpu as pltpu
from jax.sharding import PartitionSpec as P

ROWS = 160
NLON = 320
CHAN = 128
HIDDEN = 256
FORCE = 8
FIRES = 256
NS = 16
JL = 10
HB = 5
MM = 10
FULL = 200
PARTS = ((0, 2, 40), (2, 3, 64))
ROW_PARTS = ((0, 8), (80, 12))
OPERANDS = 16
FAR_FIRST = (4, 12, 5, 11, 3, 13, 6, 10, 2, 14, 7, 9, 1, 15, 8)
OWNERS = 5
EPSILON = 1e-06
MESH = pl.DeviceIdType.MESH
F32 = jnp.float32
BF16 = jnp.bfloat16
ROOT = math.sqrt(2.0 / math.pi)
CUBIC = 0.044715


def constant_tables():
    device = np.arange(NS)
    low = 5 * device[None, :] + np.arange(HB)[:, None]
    orders = np.stack([low, ROWS - 1 - low])
    flat = orders.reshape(-1)
    angle = 2.0 * np.pi * ((flat[:, None] * np.arange(NLON)[None, :]) % NLON) / NLON
    cosine, sine = np.cos(angle), np.sin(angle)
    factor = np.where(flat == 0, 1.0, 2.0)[:, None]
    analysis = np.concatenate([cosine, -sine], axis=0) / NLON
    synthesis = np.concatenate([factor * cosine, -factor * sine], axis=0)
    theta = np.pi * (np.arange(ROWS) + 0.5) / ROWS
    start = np.zeros((NS, 16, 256))
    for d in range(NS):
        for r in range(MM):
            m = float(orders[r // HB, r % HB, d])
            log_start = (
                0.5 * math.log((2.0 * m + 1.0) / (4.0 * math.pi))
                + 0.5 * (math.lgamma(m + 0.5) - math.lgamma(m + 1.0))
                - 0.25 * math.log(math.pi)
            )
            start[d, r, :ROWS] = np.exp(log_start + m * np.log(np.sin(theta)))
    waves = np.zeros((8, 256))
    waves[0, :ROWS] = np.cos(theta)
    waves[1, :ROWS] = 2.0 * np.pi * np.pi / ROWS * np.sin(theta)
    narrow = lambda t: np.ascontiguousarray(t).astype(np.float32).astype(ml_dtypes.bfloat16)
    return (
        narrow(analysis),
        narrow(analysis.T),
        narrow(synthesis),
        narrow(synthesis.T),
        start.astype(np.float32),
        waves.astype(np.float32),
    )


def mm_nn(a, b):
    return lax.dot_general(a, b, (((1,), (0,)), ((), ())), preferred_element_type=F32)


def mm_nt(a, b):
    return lax.dot_general(a, b, (((1,), (1,)), ((), ())), preferred_element_type=F32)


def mm_tn(a, b):
    return lax.dot_general(a, b, (((0,), (0,)), ((), ())), preferred_element_type=F32)


def mm_exact(a, b):
    return lax.dot_general(
        a, b, (((1,), (0,)), ((), ())), preferred_element_type=F32, precision=lax.Precision.HIGHEST
    )


def mean(values):
    return jnp.sum(values, axis=-1, keepdims=True) * (1.0 / CHAN)


def normalize(values):
    centre = values - mean(values)
    scale = lax.rsqrt(mean(centre * centre) + EPSILON)
    return centre * scale, scale


def normalize_grad(unit, scale, grad):
    return scale * (grad - mean(grad) - unit * mean(grad * unit))


def gelu_parts(v):
    square = v * v
    t = jnp.tanh(ROOT * v * (1.0 + CUBIC * square))
    half = 0.5 * (1.0 + t)
    slope = half + 0.5 * v * (1.0 - t * t) * (ROOT * (1.0 + 3.0 * CUBIC * square))
    return v * half, slope


def wide(a, b):
    return jnp.concatenate([a, b], axis=-1)


def loop(count, body, start=0):
    def step(index, carry):
        body(index)
        return carry

    lax.fori_loop(start, count, step, 0)


def unrolled(count, body, start=0):
    for index in range(start, count):
        body(index)


def rounded(v):
    return v.astype(BF16).astype(F32)


def step_kernel(nd, *refs):
    outside, results = refs[:OPERANDS], refs[OPERANDS : OPERANDS + 6]
    inside, sems = refs[OPERANDS + 6 : 2 * OPERANDS + 6], refs[2 * OPERANDS + 6]
    copies = [
        pltpu.make_async_copy(outside[n], inside[n], sems.at[n]) for n in range(OPERANDS)
    ]
    for copy in copies:
        copy.start()

    def ready(first, last):
        for copy in copies[first:last]:
            copy.wait()

    step_body(nd, ready, *inside, *results, *refs[2 * OPERANDS + 7 :])


def step_body(
    nd,
    ready,
    x_ref,
    cells_row,
    kinds_row,
    heat_row,
    table_ref,
    ana_ref,
    start_ref,
    waves_ref,
    weight_ref,
    cot_ref,
    synt_ref,
    skip_ref,
    up_ref,
    down_ref,
    syn_ref,
    anat_ref,
    field_out,
    spectral_out,
    skip_out,
    up_out,
    down_out,
    table_out,
    unit,
    scale,
    normed,
    inner_grad,
    fire_g,
    fire_t,
    taken,
    made,
    fsend,
    frecv,
    hsend_a,
    hrecv_a,
    hsend_b,
    hrecv_b,
    extra,
    back_a,
    back_b,
    t0,
    t1,
    plain,
    weighted,
    mix,
    coef_a,
    coef_b,
    grad_a,
    grad_b,
    small,
    small_in,
    piece1,
    own_in,
    own_sum,
    piece2,
    small_all,
    spec,
    spec_send,
    spec_core,
    spec_mine,
    spec_in,
    spec_piece,
    spec_all,
    tab_mine,
    tab_space,
    tab_sum,
    tab_dp,
    ssem,
    rsem,
    dsend,
    drecv,
):
    me = lax.axis_index("space")
    dp = lax.axis_index("dp")
    pr = 640 // nd
    sr = 1280 // max(nd // 2, 1)
    og = pr // OWNERS
    hsend, hrecv = (hsend_a, hsend_b), (hrecv_a, hrecv_b)
    back, coef, grad_rows = (back_a, back_b), (coef_a, coef_b), (grad_a, grad_b)

    barrier = pltpu.get_barrier_semaphore()

    def greet_space(o):
        pl.semaphore_signal(barrier, 1, device_id={"space": lax.rem(me + o, NS)}, device_id_type=MESH)

    def greet_dp(o):
        pl.semaphore_signal(barrier, 1, device_id={"dp": lax.rem(dp + o, nd)}, device_id_type=MESH)

    loop(NS, greet_space, 1)
    if nd > 1:
        loop(nd, greet_dp, 1)

    def exchange(send, recv, at, k, source):
        count = at.size
        for e in range(NS):
            send[e, at, :] = made[pl.ds(pl.multiple_of(source(e), 8), count), :].astype(BF16)
        for o in FAR_FIRST:
            e = lax.rem(me + o, NS)
            pltpu.make_async_remote_copy(
                src_ref=send.at[e, at],
                dst_ref=recv.at[me, at],
                send_sem=ssem.at[k],
                recv_sem=rsem.at[k],
                device_id={"space": e},
                device_id_type=MESH,
            ).start()
        recv[me, at, :] = send[me, at, :]

    def whole(send, recv, at, k):
        return pltpu.make_async_remote_copy(
            src_ref=send.at[pl.ds(0, NS - 1), at],
            dst_ref=recv.at[pl.ds(0, NS - 1), at],
            send_sem=ssem.at[k],
            recv_sem=rsem.at[k],
            device_id={"space": lax.rem(me + 1, NS)},
            device_id_type=MESH,
        )

    def arrived(send, recv, at, k, target):
        whole(send, recv, at, k).wait_recv()

        for s in range(NS):
            taken[pl.ds(pl.multiple_of(target(s), 8), at.size), :] = recv[s, at, :].astype(F32)

    def spread(axis, count, mine, k, source_of, recv, start):
        if count == 1:
            return
        if not start:
            done = pltpu.make_async_remote_copy(
                src_ref=recv.at[pl.ds(0, count - 1)],
                dst_ref=recv.at[pl.ds(0, count - 1)],
                send_sem=dsend.at[k],
                recv_sem=drecv.at[k],
                device_id={axis: lax.rem(mine + 1, count)},
                device_id_type=MESH,
            )
            done.wait_recv()
            done.wait_send()
            return

        def one(o):
            t = lax.rem(mine + o, count)
            pltpu.make_async_remote_copy(
                src_ref=source_of(t),
                dst_ref=recv.at[mine],
                send_sem=dsend.at[k],
                recv_sem=drecv.at[k],
                device_id={axis: t},
                device_id_type=MESH,
            ).start()

        unrolled(count, one, 1)

    def total(recv, count):
        value = recv[0].astype(F32)
        for t in range(1, count):
            value = value + recv[t].astype(F32)
        return value

    ready(0, 6)

    def column(row):
        return jnp.broadcast_to(row.astype(F32), (128, FIRES)).T

    lanes = lax.broadcasted_iota(jnp.int32, (FIRES, 128), 1)
    heat = column(heat_row[...])
    heat0 = rounded(heat)
    heat1 = rounded(heat - heat0)
    heat2 = heat - heat0 - heat1
    parts = jnp.where(lanes < 8, heat0, jnp.where(lanes < 16, heat1, heat2))
    chosen = (column(kinds_row[...]) == (lanes & 7).astype(F32)) & (lanes < 24)
    heats = jnp.where(chosen, parts, 0.0).astype(BF16)
    table_wide = table_ref[...].astype(F32)
    table3 = jnp.concatenate(
        [table_wide, table_wide, table_wide, jnp.zeros((104, CHAN), F32)], axis=0
    )

    def field_row(j):
        base = (me * JL + j) * NLON
        cells = lax.broadcasted_iota(jnp.int32, (NLON, FIRES), 0) + base
        hot = jnp.where(cells == cells_row[...], 1.0, 0.0).astype(BF16)
        fires = mm_nn(hot, heats)
        fire_g[j] = fires
        value, factor = normalize(x_ref[j].astype(F32) + mm_exact(fires, table3))
        unit[j] = value
        scale[j] = jnp.broadcast_to(factor, (NLON, CHAN))
        narrow = value.astype(BF16)
        normed[j] = narrow
        to_orders(j, ana_ref, narrow)

    def to_orders(j, table, row):
        spectrum = mm_nn(table[...], row)
        for c, (first, count, _) in enumerate(PARTS):
            start, width = ROW_PARTS[c]
            for r in range(width):
                p, h, i = r // (2 * count), r // count % 2, first + r % count
                at = (p * MM + h * HB + i) * NS
                made[pl.ds(start + j * width + r, NS, stride=FULL), :] = spectrum[at : at + NS]

    def rows_at(c, pair=None):
        start, width = ROW_PARTS[c]
        if pair is None:
            return pl.ds(start, JL * width)
        return pl.ds(pl.multiple_of(start + pair * 2 * width, 8), 2 * width)

    def send_rows(fk, k, c, pair=None):
        at = rows_at(c, pair)
        exchange(fsend.at[fk], frecv.at[fk], at, k, lambda e: e * FULL + at.start)

    def rows_arrived(fk, k, c, pair=None):
        at = rows_at(c, pair)
        start, width = ROW_PARTS[c]
        skip = NS * start - start
        arrived(
            fsend.at[fk], frecv.at[fk], at, k, lambda s: skip + s * (JL * width) + at.start
        )

    def taken_at(c, j, r):
        start, width = ROW_PARTS[c]
        return NS * start + j * width + r

    loop(2, field_row)
    pl.semaphore_wait(barrier, (NS - 1) + (nd - 1))

    def field_pair(pair):
        send_rows(0, pair, 0, pair)
        unrolled(2, lambda t: field_row(2 * pair + 2 + t))

    loop(HB - 1, field_pair)
    send_rows(0, HB - 1, 0, HB - 1)
    send_rows(0, HB, 1)

    ready(6, OPERANDS)
    row16 = lax.broadcasted_iota(jnp.int32, (16, 128), 0)
    order = jnp.where(row16 >= HB, ROWS - 1 - 5 * me - (row16 - HB), 5 * me + row16).astype(F32)
    order2 = order * order
    cos0 = jnp.broadcast_to(waves_ref[0:1, 0:128], (16, 128))
    cos1 = jnp.broadcast_to(waves_ref[0:1, 128:256], (16, 128))

    def advance(l, carry):
        p0, p1, b0, b1 = carry
        lf = jnp.full((16, 128), l, jnp.int32).astype(F32)
        lower = lf - 1.0
        upward = jnp.sqrt(
            jnp.maximum(4.0 * lf * lf - 1.0, 1.0) / jnp.maximum(lf * lf - order2, 1.0)
        )
        downward = jnp.sqrt(
            jnp.maximum(lower * lower - order2, 0.0) / jnp.maximum(4.0 * lower * lower - 1.0, 1.0)
        )
        first = start_ref[me]
        at_start = lf == order
        above = lf > order
        c0 = jnp.where(
            at_start, first[:, 0:128], jnp.where(above, upward * (cos0 * p0 - downward * b0), 0.0)
        )
        c1 = jnp.where(
            at_start, first[:, 128:256], jnp.where(above, upward * (cos1 * p1 - downward * b1), 0.0)
        )
        upper_half = l // 80
        q = l + upper_half * (ROWS - 1 - 2 * l)
        place = (upper_half * HB + q % HB) * NS + q // HB
        t0[pl.ds(place, 16, stride=ROWS), :] = c0
        t1[pl.ds(place, 16, stride=ROWS), :] = c1
        return (c0, c1, p0, p1)

    blank = start_ref[me][:, 0:128] * 0.0
    lax.fori_loop(0, ROWS, advance, (blank, blank, blank, blank))

    def narrow_tables(r):
        at = pl.ds(pl.multiple_of(r * ROWS, 8), ROWS)
        values = wide(t0[at, :], t1[at, :])
        plain[r] = values.astype(BF16)
        weighted[r] = (values * waves_ref[1:2, :]).astype(BF16)

    loop(MM, narrow_tables)

    def build_mix(g):
        real = weight_ref[2 * g]
        imag = weight_ref[2 * g + 1]
        mix[g, 0:128, 0:128] = real
        mix[g, 0:128, 128:256] = imag
        mix[g, 128:256, 0:128] = -imag
        mix[g, 128:256, 128:256] = real

    loop(2 * HB, build_mix)

    def fire_columns(j):
        fire_t[j] = fire_g[j].T[0:32]

    loop(JL, fire_columns)

    def analyse(c, k, hk, table):
        first, count, height = PARTS[c]
        rows_of = rows_of_order(c)

        def one(i):
            low = mm_nn(table[i][:, 0:ROWS], rows_of(0, i))
            high = mm_nn(table[HB + i][:, 0:ROWS], rows_of(1, i))
            for p in range(2):
                lane = slice(p * 128, (p + 1) * 128)
                for ii in range(HB):
                    ll = low[ii * NS : (ii + 1) * NS, lane]
                    lh = low[(HB + ii) * NS : (HB + ii + 1) * NS, lane]
                    hh = high[(HB + ii) * NS : (HB + ii + 1) * NS, lane]
                    at = p * 10 * count + ii * count + i - first
                    made[pl.ds(at, NS, stride=height), :] = lh
                    made[pl.ds(at + 5 * count, NS, stride=height), :] = jnp.where(row16 >= me, ll, hh)
                    extra[pl.ds(p * 32 + i * HB + ii, NS, stride=64), :] = rounded(hh)

        unrolled(first + count, one, first)
        exchange(
            hsend[c].at[hk], hrecv[c].at[hk], pl.ds(0, height), k, lambda e: e * height
        )

    def rows_of_order(c):
        first, count, _ = PARTS[c]
        _, width = ROW_PARTS[c]

        def rows(h, i):
            at = taken_at(c, 0, h * count + i - first)
            return wide(
                taken[pl.ds(at, ROWS, stride=width), :],
                taken[pl.ds(at + 2 * count, ROWS, stride=width), :],
            ).astype(BF16)

        return rows

    def mix_degrees(c, hk_in, k_in, hk_out, k_out, backward):
        first, count, height = PARTS[c]
        n = count * NS
        at = pl.ds(0, height)
        arrived(hsend[c].at[hk_in], hrecv[c].at[hk_in], at, k_in, lambda s: s * height)
        product = mm_nt if backward else mm_nn
        from_low = (lax.broadcasted_iota(jnp.int32, (n, 256), 0) & 15) <= me
        for ii in range(HB):

            def gather(slot):
                pieces = []
                for i in range(count):
                    r = slot * 5 * count + ii * count + i
                    pieces.append(
                        wide(
                            taken[pl.ds(r, NS, stride=height), :],
                            taken[pl.ds(10 * count + r, NS, stride=height), :],
                        )
                    )
                return jnp.concatenate(pieces, axis=0)

            own = wide(
                extra[pl.ds(me * 64 + first * HB + ii, 8, stride=HB), :],
                extra[pl.ds(me * 64 + 32 + first * HB + ii, 8, stride=HB), :],
            )
            own = jnp.where(lax.broadcasted_iota(jnp.int32, (8, 256), 0) < count, own, 0.0)
            second = gather(1)
            rows = jnp.concatenate([gather(0), second, own, jnp.zeros((8, 256), F32)], axis=0)
            narrow = rows.astype(BF16)
            high = product(narrow, mix[HB + ii])
            low = product(second.astype(BF16), mix[ii])
            mixed_second = jnp.where(from_low, low, high[n : 2 * n])
            for p in range(2):
                lane = slice(p * 128, (p + 1) * 128)
                for i in range(count):
                    r = p * 10 * count + ii * count + i
                    piece = slice(i * NS, (i + 1) * NS)
                    made[pl.ds(r, NS, stride=height), :] = high[piece, lane]
                    made[pl.ds(r + 5 * count, NS, stride=height), :] = mixed_second[piece, lane]
                at_own = p * 32 + ii * count
                back[c][at_own : at_own + 8, :] = rounded(high[2 * n : 2 * n + 8, lane])
            if backward:
                grad_rows[c][ii] = narrow
            else:
                coef[c][ii] = narrow
        exchange(hsend[c].at[hk_out], hrecv[c].at[hk_out], at, k_out, lambda e: e * height)

    def weight_gradient(ii):
        grad_low = jnp.zeros((256, 256), F32)
        grad_high = jnp.zeros((256, 256), F32)
        for c, (_, count, _) in enumerate(PARTS):
            n = count * NS
            kept = coef[c][ii].astype(F32)
            others = grad_rows[c][ii]
            from_low = (lax.broadcasted_iota(jnp.int32, (n, 256), 0) & 15) <= me
            second = kept[n : 2 * n]
            kept_high = jnp.concatenate(
                [kept[0:n], jnp.where(from_low, 0.0, second), kept[2 * n : 2 * n + 16]], axis=0
            )
            kept_low = jnp.where(from_low, second, 0.0)
            grad_high = grad_high + mm_tn(kept_high.astype(BF16), others)
            grad_low = grad_low + mm_tn(kept_low.astype(BF16), others[n : 2 * n])
        for half, grad in ((0, grad_low), (1, grad_high)):
            at = pl.multiple_of((half * HB + ii) * 256, 256)
            spec[pl.ds(at, 128), :] = grad[0:128, 0:128] + grad[128:256, 128:256]
            spec[pl.ds(at + 128, 128), :] = grad[0:128, 128:256] - grad[128:256, 0:128]

    def synthesise(c, hk, k_in, table):
        first, count, height = PARTS[c]
        _, width = ROW_PARTS[c]
        arrived(
            hsend[c].at[hk], hrecv[c].at[hk], pl.ds(0, height), k_in, lambda s: s * height
        )

        def one(i):
            def rows_of(slot, ii):
                r = slot * 5 * count + ii * count + i - first
                return wide(
                    taken[pl.ds(r, NS, stride=height), :],
                    taken[pl.ds(10 * count + r, NS, stride=height), :],
                )

            seconds = [rows_of(1, ii) for ii in range(HB)]
            firsts = [rows_of(0, ii) for ii in range(HB)]
            mine = lax.broadcasted_iota(jnp.int32, (NS, 256), 0) == me
            highs = []
            for ii in range(HB):
                r = ii * count + i - first
                own = wide(back[c][pl.ds(r, 1), :], back[c][pl.ds(32 + r, 1), :])
                highs.append(jnp.where(mine, jnp.broadcast_to(own, (NS, 256)), seconds[ii]))
            low = mm_tn(
                table[i][:, 0:ROWS], jnp.concatenate(seconds + firsts, axis=0).astype(BF16)
            )
            high = mm_tn(
                table[HB + i][:, 0:ROWS], jnp.concatenate(seconds + highs, axis=0).astype(BF16)
            )
            for p in range(2):
                lane = slice(p * 128, (p + 1) * 128)
                at = taken_at(c, 0, p * 2 * count + i - first)
                made[pl.ds(at, ROWS, stride=width), :] = low[:, lane]
                made[pl.ds(at + count, ROWS, stride=width), :] = high[:, lane]

        unrolled(first + count, one, first)

    def send_back(fk, k, c, pair=None):
        at = rows_at(c, pair)
        start, width = ROW_PARTS[c]
        skip = NS * start - start
        exchange(
            fsend.at[fk], frecv.at[fk], at, k, lambda e: skip + e * (JL * width) + at.start
        )

    def from_orders(j, table):
        pieces = []
        for p in range(2):
            for h in range(2):
                for c, (_, count, _) in enumerate(PARTS):
                    _, width = ROW_PARTS[c]
                    for i in range(count):
                        at = taken_at(c, j, (p * 2 + h) * count + i)
                        pieces.append(taken[pl.ds(at, NS, stride=JL * width), :])
        return mm_nn(table[...], jnp.concatenate(pieces, axis=0).astype(BF16))

    def orders_arrived(fk, k, c):
        if c == 0:
            loop(HB, lambda pair: rows_arrived(fk, k + pair, 0, pair))
        else:
            rows_arrived(fk, k + HB, 1)

    for c in range(2):
        orders_arrived(0, 0, c)
        analyse(c, 6 + c, 0, weighted)
    for c in range(2):
        mix_degrees(c, 0, 6 + c, 1, 8 + c, False)
    synthesise(0, 1, 8, plain)
    send_back(1, 10, 0)
    synthesise(1, 1, 9, plain)
    loop(HB, lambda pair: send_back(1, 11 + pair, 1, pair))

    small[...] = jnp.zeros((640, CHAN), F32)

    def middle_row(j):
        row = normed[j]
        inner = from_orders(j, synt_ref) + mm_nn(row, skip_ref[...])
        activated, inner_slope = gelu_parts(inner)
        second, factor = normalize(activated)
        narrow = second.astype(BF16)
        upper = mm_nn(narrow, up_ref[...])
        hidden, slope = gelu_parts(upper)
        incoming = cot_ref[j]
        grad_upper = (mm_nt(incoming, down_ref[...]) * slope).astype(BF16)
        grad_second = mm_nt(grad_upper, up_ref[...])
        small[384:640, :] += mm_tn(hidden.astype(BF16), incoming)
        grad_up = mm_tn(narrow, grad_upper)
        small[128:256, :] += grad_up[:, 0:128]
        small[256:384, :] += grad_up[:, 128:256]
        grad_inner = (normalize_grad(second, factor, grad_second) * inner_slope).astype(BF16)
        small[0:128, :] += mm_tn(row, grad_inner)
        inner_grad[j] = grad_inner
        to_orders(j, syn_ref, grad_inner)

    rows_arrived(1, 10, 0)

    def middle_pair(pair):
        rows_arrived(1, 11 + pair, 1, pair)
        unrolled(2, lambda t: middle_row(2 * pair + t))
        send_rows(2, 16 + pair, 0, pair)

    loop(HB, middle_pair)
    send_rows(2, 16 + HB, 1)

    def small_source(t):
        return small.at[pl.ds(pl.multiple_of(t * pr, 8), pr), :]

    spread("dp", nd, dp, 0, small_source, small_in, True)
    small_in[dp] = small[pl.ds(pl.multiple_of(dp * pr, 8), pr), :]

    for c in range(2):
        orders_arrived(2, 16, c)
        analyse(c, 22 + c, 2, plain)

    spread("dp", nd, dp, 0, small_source, small_in, False)
    piece1[...] = total(small_in, nd)

    def owner_copy(e, slot):
        return pltpu.make_async_remote_copy(
            src_ref=piece1.at[pl.ds(pl.multiple_of(e * og, 8), og)],
            dst_ref=own_in.at[slot],
            send_sem=dsend.at[1],
            recv_sem=drecv.at[1],
            device_id={"space": e},
            device_id_type=MESH,
        )

    def to_owner(e):
        @pl.when(e != me)
        def _():
            owner_copy(e, me).start()

    loop(OWNERS, to_owner)

    for c in range(2):
        mix_degrees(c, 2, 22 + c, 3, 24 + c, True)

    def owner_out(t, slot):
        return pltpu.make_async_remote_copy(
            src_ref=own_sum,
            dst_ref=piece2.at[slot],
            send_sem=dsend.at[2],
            recv_sem=drecv.at[2],
            device_id={"space": t},
            device_id_type=MESH,
        )

    @pl.when(me < OWNERS)
    def _():
        own_in[me] = piece1[pl.ds(pl.multiple_of(me * og, 8), og), :]
        gathered = pltpu.make_async_remote_copy(
            src_ref=own_in.at[pl.ds(0, NS - 1)],
            dst_ref=own_in.at[pl.ds(0, NS - 1)],
            send_sem=dsend.at[1],
            recv_sem=drecv.at[1],
            device_id={"space": lax.rem(me + 1, NS)},
            device_id_type=MESH,
        )
        gathered.wait_recv()
        own_sum[...] = total(own_in, NS)
        piece2[me] = own_sum[...]

        def tell(o):
            owner_out(lax.rem(me + o, NS), me).start()

        loop(NS, tell, 1)

    loop(HB, weight_gradient)

    half = 1280
    nq = nd // 2
    core = lax.rem(dp, 2)
    chip = dp // 2

    def to_core(source, target, k):
        return pltpu.make_async_remote_copy(
            src_ref=source,
            dst_ref=target,
            send_sem=dsend.at[k],
            recv_sem=drecv.at[k],
            device_id={"dp": dp + 1 - 2 * core},
            device_id_type=MESH,
        )

    def to_chips(source_of, recv, k, start):
        if nq <= 1:
            return
        if not start:
            done = to_core(recv.at[pl.ds(0, nq - 1)], recv.at[pl.ds(0, nq - 1)], k)
            done.wait_recv()
            done.wait_send()
            return

        def one(o):
            t = lax.rem(chip + o, nq)
            pltpu.make_async_remote_copy(
                src_ref=source_of(t),
                dst_ref=recv.at[chip],
                send_sem=dsend.at[k],
                recv_sem=drecv.at[k],
                device_id={"dp": 2 * t + core},
                device_id_type=MESH,
            ).start()

        loop(nq, one, 1)

    def spec_first():
        if nd == 1:
            return
        other = pl.multiple_of((1 - core) * half, 128)
        spec_send[...] = spec[pl.ds(other, half), :].astype(BF16)
        to_core(spec_send, spec_core, 3).start()

    def spec_second():
        if nd == 1:
            return
        to_core(spec_send, spec_core, 3).wait_recv()
        mine = pl.multiple_of(core * half, 128)

        def add(t):
            at = pl.ds(pl.multiple_of(t * sr, 16), sr)
            both = spec[pl.ds(pl.multiple_of(mine + t * sr, 16), sr), :] + spec_core[at, :].astype(F32)
            spec_mine[t] = both.astype(BF16)

        loop(nq, add)
        to_chips(lambda t: spec_mine.at[t], spec_in, 5, True)
        spec_in[chip] = spec_mine[chip]

    def spec_third():
        if nd == 1:
            return
        to_core(spec_send, spec_core, 3).wait_send()
        to_chips(lambda t: spec_mine.at[t], spec_in, 5, False)
        spec_piece[...] = total(spec_in, nq).astype(BF16)
        to_chips(lambda t: spec_piece, spec_all.at[core], 6, True)
        spec_all[core, chip] = spec_piece[...]

    def spec_fourth():
        if nd == 1:
            return
        to_chips(lambda t: spec_piece, spec_all.at[core], 6, False)
        to_core(spec_all.at[core], spec_all.at[core], 7).start()

    def spec_fifth():
        if nd == 1:
            spectral_out[...] = spec[...]
            return
        to_core(spec_all.at[core], spec_all.at[1 - core], 7).wait()

        def widen(t):
            for c in range(2):
                at = pl.ds(pl.multiple_of(c * half + t * sr, 16), sr)
                spectral_out[at, :] = spec_all[c, t].astype(F32)

        loop(nq, widen)

    spec_first()
    synthesise(0, 3, 24, weighted)
    send_back(3, 26, 0)
    spec_second()
    synthesise(1, 3, 25, weighted)
    loop(HB, lambda pair: send_back(3, 27 + pair, 1, pair))

    def counted(ref, count, k):
        return pltpu.make_async_remote_copy(
            src_ref=ref.at[pl.ds(0, count)],
            dst_ref=ref.at[pl.ds(0, count)],
            send_sem=dsend.at[k],
            recv_sem=drecv.at[k],
            device_id={"space": lax.rem(me + 1, NS)},
            device_id_type=MESH,
        )

    @pl.when(me < OWNERS)
    def _():
        counted(own_in, OWNERS - 1, 1).wait_send()
        counted(piece2, OWNERS - 1, 2).wait_recv()
        counted(own_in, NS - 1, 2).wait_send()

    @pl.when(me >= OWNERS)
    def _():
        counted(own_in, OWNERS, 1).wait_send()
        counted(piece2, OWNERS, 2).wait_recv()

    spread("dp", nd, dp, 4, lambda t: piece2, small_all, True)
    small_all[dp] = piece2[...]

    spec_third()

    for k, fk in ((0, 0), (16, 2)):
        loop(HB, lambda pair: whole(fsend.at[fk], frecv.at[fk], rows_at(0, pair), k + pair).wait_send())
        whole(fsend.at[fk], frecv.at[fk], rows_at(1), k + HB).wait_send()
    for k, hk in ((6, 0), (8, 1), (22, 2), (24, 3)):
        for c, (_, _, height) in enumerate(PARTS):
            whole(hsend[c].at[hk], hrecv[c].at[hk], pl.ds(0, height), k + c).wait_send()

    def back_sent(k, fk):
        whole(fsend.at[fk], frecv.at[fk], rows_at(0), k).wait_send()
        loop(HB, lambda pair: whole(fsend.at[fk], frecv.at[fk], rows_at(1, pair), k + 1 + pair).wait_send())

    back_sent(10, 1)

    tab_mine[...] = jnp.zeros((32, CHAN), F32)

    def last_row(j):
        grad_normed = from_orders(j, anat_ref) + mm_nt(inner_grad[j], skip_ref[...])
        grad = cot_ref[j].astype(F32) + normalize_grad(unit[j], scale[j], grad_normed)
        field_out[j] = grad.astype(BF16)
        tab_mine[...] += mm_exact(fire_t[j], grad)

    rows_arrived(3, 26, 0)

    def last_pair(pair):
        rows_arrived(3, 27 + pair, 1, pair)
        unrolled(2, lambda t: last_row(2 * pair + t))

    loop(3, last_pair)
    spec_fourth()
    loop(HB, last_pair, 3)
    tab_mine[0:8, :] = tab_mine[0:8, :] + tab_mine[8:16, :] + tab_mine[16:24, :]
    spread("space", NS, me, 8, lambda t: tab_mine.at[0:8], tab_space, True)
    tab_space[me] = tab_mine[0:8, :]

    back_sent(26, 3)
    spread("dp", nd, dp, 4, lambda t: piece2, small_all, False)
    flat_small = [small_all[t, g] for t in range(nd) for g in range(OWNERS)]
    flat_small = jnp.concatenate(flat_small, axis=0)
    skip_out[...] = flat_small[0:128]
    up_out[:, 0:128] = flat_small[128:256]
    up_out[:, 128:256] = flat_small[256:384]
    down_out[...] = flat_small[384:640]
    spec_fifth()

    spread("space", NS, me, 8, lambda t: tab_mine.at[0:8], tab_space, False)
    tab_sum[...] = total(tab_space, NS)
    spread("dp", nd, dp, 9, lambda t: tab_sum, tab_dp, True)
    tab_dp[dp] = tab_sum[...]
    spread("dp", nd, dp, 9, lambda t: tab_sum, tab_dp, False)
    table_out[...] = total(tab_dp, nd)


def hand_over(*refs):
    sems = refs[-1]
    count = len(refs) // 2
    copies = [
        pltpu.make_async_copy(refs[n], refs[count + n], sems.at[n]) for n in range(count)
    ]
    for copy in copies:
        copy.start()
    for copy in copies:
        copy.wait()


def shards(
    nd,
    state_field,
    cotangent,
    fire_cells,
    fire_kinds,
    fire_heat,
    forcing_table,
    spectral_weight,
    skip_weight,
    up_weight,
    down_weight,
):
    ana, anat, syn, synt, start, waves = (jnp.asarray(t) for t in constant_tables())
    nq = max(nd // 2, 1)
    pr, sr = 640 // nd, 1280 // nq
    operands = (
        state_field[0],
        fire_cells,
        fire_kinds,
        fire_heat,
        forcing_table,
        ana,
        start,
        waves,
        spectral_weight.reshape(4 * HB, CHAN, CHAN),
        cotangent[0],
        synt,
        skip_weight,
        up_weight,
        down_weight,
        syn,
        anat,
    )
    vmem = pl.BlockSpec(memory_space=pltpu.VMEM)
    out_shape = (
        jax.ShapeDtypeStruct((JL, NLON, CHAN), BF16),
        jax.ShapeDtypeStruct((2560, CHAN), F32),
        jax.ShapeDtypeStruct((CHAN, CHAN), F32),
        jax.ShapeDtypeStruct((CHAN, HIDDEN), F32),
        jax.ShapeDtypeStruct((HIDDEN, CHAN), F32),
        jax.ShapeDtypeStruct((FORCE, CHAN), F32),
    )
    (_, ca, ha), (_, cb, hb) = PARTS
    outside = pl.BlockSpec(memory_space=pltpu.HBM)
    scratch = [pltpu.VMEM(v.shape, v.dtype) for v in operands]
    scratch += [
        pltpu.SemaphoreType.DMA((OPERANDS,)),
        pltpu.VMEM((JL, NLON, CHAN), F32),
        pltpu.VMEM((JL, NLON, CHAN), F32),
        pltpu.VMEM((JL, NLON, CHAN), BF16),
        pltpu.VMEM((JL, NLON, CHAN), BF16),
        pltpu.VMEM((JL, NLON, CHAN), F32),
        pltpu.VMEM((JL, 32, NLON), F32),
        pltpu.VMEM((NS * FULL, CHAN), F32),
        pltpu.VMEM((NS * FULL, CHAN), F32),
        pltpu.VMEM((4, NS, FULL, CHAN), BF16),
        pltpu.VMEM((4, NS, FULL, CHAN), BF16),
        pltpu.VMEM((4, NS, ha, CHAN), BF16),
        pltpu.VMEM((4, NS, ha, CHAN), BF16),
        pltpu.VMEM((4, NS, hb, CHAN), BF16),
        pltpu.VMEM((4, NS, hb, CHAN), BF16),
        pltpu.VMEM((NS * 64 + 32, CHAN), F32),
        pltpu.VMEM((64, CHAN), F32),
        pltpu.VMEM((64, CHAN), F32),
        pltpu.VMEM((16 * ROWS, 128), F32),
        pltpu.VMEM((16 * ROWS, 128), F32),
        pltpu.VMEM((MM, ROWS, 256), BF16),
        pltpu.VMEM((MM, ROWS, 256), BF16),
        pltpu.VMEM((2 * HB, 256, 256), BF16),
        pltpu.VMEM((HB, 2 * NS * ca + 16, 256), BF16),
        pltpu.VMEM((HB, 2 * NS * cb + 16, 256), BF16),
        pltpu.VMEM((HB, 2 * NS * ca + 16, 256), BF16),
        pltpu.VMEM((HB, 2 * NS * cb + 16, 256), BF16),
        pltpu.VMEM((640, CHAN), F32),
        pltpu.VMEM((nd, pr, CHAN), F32),
        pltpu.VMEM((pr, CHAN), F32),
        pltpu.VMEM((NS, pr // OWNERS, CHAN), F32),
        pltpu.VMEM((pr // OWNERS, CHAN), F32),
        pltpu.VMEM((OWNERS, pr // OWNERS, CHAN), F32),
        pltpu.VMEM((nd, OWNERS, pr // OWNERS, CHAN), F32),
        pltpu.VMEM((2560, CHAN), F32),
        pltpu.VMEM((1280, CHAN), BF16),
        pltpu.VMEM((1280, CHAN), BF16),
        pltpu.VMEM((nq, sr, CHAN), BF16),
        pltpu.VMEM((nq, sr, CHAN), BF16),
        pltpu.VMEM((sr, CHAN), BF16),
        pltpu.VMEM((2, nq, sr, CHAN), BF16),
        pltpu.VMEM((32, CHAN), F32),
        pltpu.VMEM((NS, FORCE, CHAN), F32),
        pltpu.VMEM((FORCE, CHAN), F32),
        pltpu.VMEM((nd, FORCE, CHAN), F32),
        pltpu.SemaphoreType.DMA((32,)),
        pltpu.SemaphoreType.DMA((32,)),
        pltpu.SemaphoreType.DMA((10,)),
        pltpu.SemaphoreType.DMA((10,)),
    ]
    results = pl.pallas_call(
        functools.partial(step_kernel, nd),
        out_shape=out_shape,
        in_specs=[outside] * len(operands),
        out_specs=(vmem,) * len(out_shape),
        scratch_shapes=scratch,
        compiler_params=pltpu.CompilerParams(
            collective_id=0, has_side_effects=True, vmem_limit_bytes=60 << 20
        ),
        name="step",
    )(*operands)
    hbm = pl.BlockSpec(memory_space=pl.ANY)
    field, spectral, skip, up, down, table = pl.pallas_call(
        hand_over,
        out_shape=out_shape,
        in_specs=[vmem] * len(out_shape),
        out_specs=(hbm,) * len(out_shape),
        scratch_shapes=[pltpu.SemaphoreType.DMA((len(out_shape),))],
        name="hand_over",
    )(*results)
    return (field[None], spectral.reshape(spectral_weight.shape), skip, up, down, table)


def solution(mesh):
    return jax.shard_map(
        functools.partial(shards, mesh.shape["dp"]),
        mesh=mesh,
        in_specs=(
            P("dp", "space", None, None),
            P("dp", "space", None, None),
            P("dp", None),
            P("dp", None),
            P("dp", None),
            P(),
            P(None, "space", None, None, None),
            P(),
            P(),
            P(),
        ),
        out_specs=(
            P("dp", "space", None, None),
            P(None, "space", None, None, None),
            P(),
            P(),
            P(),
            P(),
        ),
        check_vma=False,
    )
```
